128 devices in a mesh: tile: 16 (over x_lo, z, core), chan: 8 (over y, x_hi).
Axes of the slice: x: 4 (x_hi: 2, x_lo: 2; x = x_hi * 2 + x_lo), y: 4, z: 4, core: 2. Of those that a mesh axis runs over, the one named last changes fastest.
Arguments:
- voltages: int32 [512, 262144], P('tile', 'chan'), may hold values from -128 to 127
- history: int32 [512, 30720], P('tile'), may hold values from -128 to 127
- filter_taps: int32 [16, 2048], replicated, may hold values from -64 to 64
Outputs:
- visibilities: float32 [2, 1024, 512, 512], P(None, 'chan', 'tile')
The draws below stay inside these ranges and needn't reach their ends.
Inputs may be any that keep to these rules, and one draw needn't show every extreme that they name: `voltages`: 8-bit signed samples. `history`: 8-bit signed samples.
All inputs are finite; a program needn't handle non-finite values.
Results may differ from the reference program's by a relative error of at most 0.006.
Values may be sent and summed in bfloat16 or wider, within the bound.
A program may use at most 192 MiB of HBM per device.

```python
import math
import jax
import jax.numpy as jnp
from jax import lax

CH = 1024
TAPS = 16
INPUTS = 512
FFT = 2048
SPEC = 128


def plant(values, stream_key, smallest, high):
    place = [jax.random.randint(jax.random.fold_in(stream_key, axis), (), 0, length) for axis, length in enumerate(values.shape)]
    main_axis = values.shape.index(max(values.shape))
    next_to = place[:main_axis] + [(place[main_axis] + 1) % values.shape[main_axis]] + place[main_axis + 1:]
    return values.at[tuple(place)].set(smallest).at[tuple(next_to)].set(high)


def setup_inputs(seed: int = 0) -> dict:
    keys = jax.random.split(jax.random.key(seed), 4)
    return {
        "voltages": plant(jax.random.randint(keys[0], (INPUTS, SPEC * FFT), -128, 128), jax.random.fold_in(keys[0], 1), -128, 127).astype(jnp.int32),
        "history": plant(jax.random.randint(keys[1], (INPUTS, (TAPS - 1) * FFT), -128, 128), jax.random.fold_in(keys[1], 1), -128, 127).astype(jnp.int32),
        "filter_taps": plant(jax.random.randint(keys[2], (TAPS, FFT), -64, 65), jax.random.fold_in(keys[2], 1), -64, 64).astype(jnp.int32),
    }


filter_norm = 1.0 / 16384.0

def dft_table(samples, channels):
    rows_index = jnp.arange(samples, dtype=jnp.int32)[:, None]
    cols_index = jnp.arange(channels, dtype=jnp.int32)[None, :]
    angles = (rows_index * cols_index % samples).astype(jnp.float32) * (2.0 * math.pi / samples)
    factor = 1.0 / math.sqrt(channels)
    return jnp.concatenate([jnp.cos(angles) * factor, -jnp.sin(angles) * factor], axis=1).astype(jnp.bfloat16)

def polyphase(extended, weights, spectra_count):
    summed = jnp.zeros((extended.shape[0], spectra_count, extended.shape[2]), jnp.float32)
    for tap_index in range(weights.shape[0]):
        summed = summed + weights[tap_index][None, None, :] * extended[:, tap_index:tap_index + spectra_count, :]
    return summed

def counter_rows(spectra):
    real_part = spectra[:, :, 0]
    imag_part = spectra[:, :, 1]
    rotated = jnp.stack([imag_part, -real_part], axis=2)
    return jnp.stack([spectra, rotated], axis=0)

def reference(voltages, history, filter_taps):
    inputs_all = voltages.shape[0]
    spectra_count = voltages.shape[1] // FFT
    extended = jnp.concatenate([history.astype(jnp.float32), voltages.astype(jnp.float32)], axis=1)
    extended = extended.reshape(inputs_all, spectra_count + TAPS - 1, FFT)
    filtered = (polyphase(extended, filter_taps.astype(jnp.float32), spectra_count) * filter_norm).astype(jnp.bfloat16)
    spectra = jnp.dot(filtered.reshape(-1, FFT), dft_table(FFT, CH), preferred_element_type=jnp.float32)
    spectra = spectra.reshape(inputs_all, spectra_count, 2, CH).astype(jnp.bfloat16)
    width_block = math.gcd(CH, 64)
    block_count = CH // width_block
    grouped = spectra.reshape(inputs_all, spectra_count, 2, block_count, width_block).transpose(3, 0, 1, 2, 4).astype(jnp.float32)
    average = 1.0 / spectra_count

    def one_block(channel_part):
        stacked = counter_rows(channel_part)
        return jnp.einsum('qaspc,bspc->qcab', stacked, channel_part) * average
    results = lax.map(one_block, grouped)
    return results.transpose(1, 0, 2, 3, 4).reshape(2, CH, inputs_all, inputs_all)
```

```python
import functools
import math

import jax
import jax.numpy as jnp
import numpy as np
from jax import lax
from jax.experimental import pallas as pl
from jax.experimental.pallas import tpu as pltpu
from jax.sharding import PartitionSpec as P

CH = 1024
TAPS = 16
FFT = 2048
SPEC = 128
INPUTS = 512

NT = FFT // 128
CHAN = 8
ROWS = 32
OWN = ROWS // CHAN
SLOC = SPEC // CHAN
KD = 32
CK = 4
NCH = KD // CK
AHEAD = 2

MESH = pl.DeviceIdType.MESH
F32 = jnp.float32
BF16 = jnp.bfloat16


def phase_tables():
    k = np.arange(CH, dtype=np.int64)
    fine = (k[:, None] * np.arange(128)[None, :]) % FFT * (2.0 * math.pi / FFT)
    fine = np.stack([np.cos(fine), np.sin(fine)]) / math.sqrt(CH)
    coarse = (np.arange(NT)[:, None] * np.arange(16)[None, :]) % 16 * (2.0 * math.pi / 16)
    coarse = np.stack([np.cos(coarse), np.sin(coarse)])
    coarse = np.broadcast_to(coarse[..., None], (2, NT, 16, 128))
    return fine.astype(np.float32), np.ascontiguousarray(coarse).astype(np.float32)


def place():
    tile, chan = lax.axis_index("tile"), lax.axis_index("chan")
    x_lo, z, core = tile // 8, (tile // 2) % 4, tile % 2
    return tile, chan, x_lo, z, core


def plane_tile(q, z):
    return (q // 2) * 8 + z * 2 + q % 2


def front_kernel(
    volt, hist, taps, fine, coarse, got,
    h8, table, pack, hpack, send, recv, ext, filt, fir, spec, out2,
    hsem, s1, r1, s2, r2, lsem,
):
    tile, chan, x_lo, z, core = place()
    q = x_lo * 2 + core
    hcopy = pltpu.make_async_copy(
        hist.at[pl.ds(pl.multiple_of((chan // 2) * 8, 8), 8), :], h8, hsem
    )
    hcopy.start()

    barrier = pltpu.get_barrier_semaphore()

    @pl.loop(1, 32)
    def _(i):
        other = lax.rem(q * 8 + chan + i, 32)
        pl.semaphore_signal(
            barrier, inc=1, device_id=(plane_tile(other // 8, z), other % 8), device_id_type=MESH
        )

    @pl.loop(0, NT)
    def _(nt):
        for s in range(SLOC):
            lanes = pl.ds(pl.multiple_of(s * FFT + nt * 128, 128), 128)
            pack[pl.ds(s, ROWS, stride=SLOC), :] = volt[:, lanes].astype(F32)
        for c in range(CHAN):
            send[c, nt] = pack[pl.ds(c * OWN * SLOC, OWN * SLOC), :].astype(BF16)

    pl.semaphore_wait(barrier, 31)

    def first(i):
        to = lax.rem(chan + i, CHAN)
        return pltpu.make_async_remote_copy(
            src_ref=send.at[to], dst_ref=recv.at[chan], send_sem=s1.at[to], recv_sem=r1.at[chan],
            device_id=(tile, to), device_id_type=MESH,
        )

    def first_in(i):
        src = lax.rem(chan + CHAN - i, CHAN)
        return pltpu.make_async_remote_copy(
            src_ref=send.at[src], dst_ref=recv.at[src], send_sem=s1.at[src], recv_sem=r1.at[src],
            device_id=(tile, src), device_id_type=MESH,
        )

    @pl.loop(1, CHAN)
    def _(i):
        first(i).start()

    recv[chan] = send[chan]
    hcopy.wait()

    @pl.loop(0, CH // 16)
    def _(kb):
        rows = pl.ds(pl.multiple_of(kb * 16, 16), 16)
        rows_im = pl.ds(pl.multiple_of(CH + kb * 16, 16), 16)
        c2, s2_ = fine[0, rows, :], fine[1, rows, :]
        for n1 in range(NT):
            c1, s1_ = coarse[0, n1], coarse[1, n1]
            lanes = pl.ds(n1 * 128, 128)
            table[rows, lanes] = (c1 * c2 - s1_ * s2_).astype(BF16)
            table[rows_im, lanes] = (-(s1_ * c2 + c1 * s2_)).astype(BF16)

    @pl.loop(1, CHAN)
    def _(i):
        first_in(i).wait_recv()

    odd = lax.rem(chan, 2)

    @pl.loop(0, NT)
    def _(nt):
        for j in range(TAPS - 1):
            lanes = pl.ds(pl.multiple_of(j * FFT + nt * 128, 128), 128)
            hpack[pl.ds(j + 1, 8, stride=16), :] = h8[:, lanes].astype(F32)
        for a in range(OWN):
            old = hpack[pl.ds(pl.multiple_of(odd * 64 + a * 16, 16), 16), :]
            ext[pl.ds(a * 2, 16, stride=8), :] = old
        for c in range(CHAN):
            for a in range(OWN):
                part = recv[c, nt, a * 16 : (a + 1) * 16, :].astype(F32)
                start = (16 + (c % 4) * 16) * 8 + a * 2 + c // 4
                ext[pl.ds(start, 16, stride=8), :] = part
                if c == 3:
                    ext[pl.ds(a * 2 + 1, 16, stride=8), :] = part
        lanes = pl.ds(pl.multiple_of(nt * 128, 128), 128)
        weights = [
            jnp.broadcast_to(taps[t : t + 1, lanes].astype(F32), (8, 128)) for t in range(TAPS)
        ]

        @pl.loop(0, 64, step=8)
        def _(j0):
            base = pl.multiple_of(j0 * 8, 64)
            rows = [ext[pl.ds(base + (r + 1) * 8, 8), :] for r in range(8 + TAPS - 1)]
            for j in range(8):
                total = weights[0] * rows[j]
                for t in range(1, TAPS):
                    total = total + weights[t] * rows[j + t]
                fir[pl.ds(j0 + j, 8, stride=64), :] = total * (1.0 / 16384.0)

        filt[:, lanes] = fir[...].astype(BF16)

    def second(i, m, kb):
        to = lax.rem(q + m, 4)
        return pltpu.make_async_remote_copy(
            src_ref=out2.at[kb, to], dst_ref=got.at[q, chan],
            send_sem=s2.at[kb, to], recv_sem=r2.at[q, chan],
            device_id=(plane_tile(to, z), kb), device_id_type=MESH,
        )

    own = pltpu.make_async_copy(out2.at[chan, q], got.at[q, chan], lsem)

    @pl.loop(0, CHAN)
    def _(i):
        kb = lax.rem(chan + 1 + i, CHAN)
        for p in range(2):
            rows = pl.ds(pl.multiple_of(p * CH + kb * 128, 128), 128)
            block = lax.dot_general(
                table[rows, :], filt[...], (((1,), (1,)), ((), ())), preferred_element_type=F32
            )
            for a in range(OWN):
                spec[pl.ds(p * OWN + a, 128, stride=8), :] = block[:, a * 128 : (a + 1) * 128]
        for to in range(4):
            out2[kb, to] = spec[pl.ds(to * 256, 256), :].astype(BF16)

        for m in (1, 2, 3):
            second(i, m, kb).start()

        @pl.when(i < CHAN - 1)
        def _():
            second(i, 0, kb).start()

    own.start()

    @pl.loop(1, CHAN)
    def _(i):
        first(i).wait_send()

    @pl.loop(1, 32)
    def _(i):
        other = lax.rem(q * 8 + chan + i, 32)
        oq, oc = other // 8, other % 8
        copy = pltpu.make_async_remote_copy(
            src_ref=out2.at[oc, oq], dst_ref=got.at[oq, oc],
            send_sem=s2.at[oc, oq], recv_sem=r2.at[oq, oc],
            device_id=(plane_tile(oq, z), oc), device_id_type=MESH,
        )
        copy.wait_send()
        copy.wait_recv()

    own.wait()


def back_kernel(
    got, out, gather, ob, sz, rz, so, ro, lsem,
):
    tile, chan, x_lo, z, core = place()
    q = x_lo * 2 + core
    up, down = lax.rem(z + 1, 4), lax.rem(z + 3, 4)
    far = lax.rem(z + 2, 4)

    barrier = pltpu.get_barrier_semaphore()
    for nz in (up, down):
        pl.semaphore_signal(
            barrier, inc=1, device_id=(plane_tile(q, nz), chan), device_id_type=MESH
        )
    for m in (1, 2, 3):
        to = lax.rem(q + m, 4)
        pl.semaphore_signal(
            barrier, inc=1, device_id=(plane_tile(to, z), chan), device_id_type=MESH
        )

    low = lax.broadcasted_iota(jnp.int32, (8, 128), 0) < 4

    @pl.loop(0, KD // 2)
    def _(kp):
        rows = pl.ds(pl.multiple_of(kp * 16, 16), 16)
        for member in range(4):
            mx, mc = member // 2, member % 2
            for half in range(2):
                parts = [got[member, half * 4 + c, rows, :].astype(F32) for c in range(4)]
                for kk in range(2):
                    v = [part[kk * 8 : kk * 8 + 8, :] for part in parts]
                    r = [pltpu.roll(x, 4, 0) for x in v]
                    re = jnp.concatenate(
                        [jnp.where(low, v[0], r[1]), jnp.where(low, v[2], r[3])], axis=0
                    )
                    im = jnp.concatenate(
                        [jnp.where(low, r[0], v[1]), jnp.where(low, r[2], v[3])], axis=0
                    )
                    at = pl.ds(mc * 32 + half * 16, 16)
                    gather[kp * 2 + kk, mx, z, at, 0:128] = re.astype(BF16)
                    gather[kp * 2 + kk, mx, z, at, 128:256] = im.astype(BF16)

    pl.semaphore_wait(barrier, 5)

    def shift(chunk, owner, to, way):
        block = gather.at[pl.ds(chunk * CK, CK), :, owner]
        return pltpu.make_async_remote_copy(
            src_ref=block, dst_ref=block, send_sem=sz.at[way, chunk], recv_sem=rz.at[way, chunk],
            device_id=(plane_tile(q, to), chan), device_id_type=MESH,
        )

    def spread(chunk, m):
        to = lax.rem(q + m, 4)
        return pltpu.make_async_remote_copy(
            src_ref=ob.at[to, :, pl.ds(chunk * CK, CK)],
            dst_ref=out.at[:, q, pl.ds(chunk * CK, CK)],
            send_sem=so.at[to, chunk], recv_sem=ro.at[q, chunk],
            device_id=(plane_tile(to, z), chan), device_id_type=MESH,
        )

    def keep(chunk):
        return pltpu.make_async_copy(
            ob.at[q, :, pl.ds(chunk * CK, CK)], out.at[:, q, pl.ds(chunk * CK, CK)],
            lsem.at[chunk],
        )

    def start_own(chunk):
        shift(chunk, z, up, 0).start()
        shift(chunk, z, down, 1).start()

    for chunk in range(AHEAD):
        start_own(chunk)

    @pl.loop(0, NCH + 1)
    def _(step):
        @pl.when(step + AHEAD < NCH)
        def _():
            start_own(step + AHEAD)

        @pl.when(step < NCH)
        def _():
            shift(step, down, up, 0).wait_recv()
            shift(step, up, down, 1).wait_recv()

            @pl.when(lax.rem(step, 2) == 0)
            def _():
                shift(step, down, up, 2).start()

            @pl.when(lax.rem(step, 2) == 1)
            def _():
                shift(step, up, down, 2).start()

        @pl.when(step > 0)
        def _():
            chunk = step - 1
            shift(chunk, far, up, 2).wait_recv()

            @pl.loop(chunk * CK, chunk * CK + CK)
            def _(k):
                mine = gather[k, :, z].reshape(128, 256)
                re, im = mine[:, :128], mine[:, 128:]
                turned = jnp.concatenate([im, -re], axis=1)
                left = jnp.concatenate([mine, turned], axis=0)
                right = gather[k].reshape(INPUTS, 256)
                vis = lax.dot_general(
                    left, right, (((1,), (1,)), ((), ())), preferred_element_type=F32
                )
                vis = (vis * (1.0 / SPEC)).astype(BF16)
                for to in range(4):
                    for p in range(2):
                        ob[to, p, k] = vis[p * 128 + to * 32 : p * 128 + to * 32 + 32, :]

            for m in (1, 2, 3):
                spread(chunk, m).start()
            keep(chunk).start()

    @pl.loop(0, NCH)
    def _(chunk):
        shift(chunk, z, up, 0).wait_send()
        shift(chunk, z, down, 1).wait_send()
        shift(chunk, far, up, 2).wait_send()
        keep(chunk).wait()
        for m in (1, 2, 3):
            spread(chunk, m).wait_send()
            src = lax.rem(q + m, 4)
            pltpu.make_async_remote_copy(
                src_ref=ob.at[src, :, pl.ds(chunk * CK, CK)],
                dst_ref=out.at[:, src, pl.ds(chunk * CK, CK)],
                send_sem=so.at[src, chunk], recv_sem=ro.at[src, chunk],
                device_id=(plane_tile(src, z), chan), device_id_type=MESH,
            ).wait_recv()


VM = pl.BlockSpec(memory_space=pltpu.VMEM)
ANY = pl.BlockSpec(memory_space=pl.ANY)
LIMIT = 60 << 20


def body(voltages, history, filter_taps):
    fine, coarse = (jnp.asarray(x) for x in phase_tables())
    got = pl.pallas_call(
        front_kernel,
        name="front",
        out_shape=jax.ShapeDtypeStruct((4, CHAN, 256, 128), BF16),
        in_specs=[VM, ANY, VM, VM, VM],
        out_specs=ANY,
        scratch_shapes=[
            pltpu.VMEM((8, (TAPS - 1) * FFT), jnp.int32),
            pltpu.VMEM((2 * CH, FFT), BF16),
            pltpu.VMEM((ROWS * SLOC, 128), F32),
            pltpu.VMEM((128, 128), F32),
            pltpu.VMEM((CHAN, NT, OWN * SLOC, 128), BF16),
            pltpu.VMEM((CHAN, NT, OWN * SLOC, 128), BF16),
            pltpu.VMEM((80 * 8, 128), F32),
            pltpu.VMEM((OWN * SPEC, FFT), BF16),
            pltpu.VMEM((OWN * SPEC, 128), F32),
            pltpu.VMEM((128 * 8, 128), F32),
            pltpu.VMEM((CHAN, 4, 256, 128), BF16),
            pltpu.SemaphoreType.DMA,
            pltpu.SemaphoreType.DMA((CHAN,)),
            pltpu.SemaphoreType.DMA((CHAN,)),
            pltpu.SemaphoreType.DMA((CHAN, 4)),
            pltpu.SemaphoreType.DMA((4, CHAN)),
            pltpu.SemaphoreType.DMA,
        ],
        compiler_params=pltpu.CompilerParams(
            collective_id=0, has_side_effects=True, vmem_limit_bytes=LIMIT
        ),
    )(voltages, history, filter_taps, fine, coarse)
    vis = pl.pallas_call(
        back_kernel,
        name="back",
        out_shape=jax.ShapeDtypeStruct((2, 4, KD, ROWS, INPUTS), BF16),
        in_specs=[VM],
        out_specs=ANY,
        scratch_shapes=[
            pltpu.VMEM((KD, 2, 4, 64, 256), BF16),
            pltpu.VMEM((4, 2, KD, ROWS, INPUTS), BF16),
            pltpu.SemaphoreType.DMA((3, NCH)),
            pltpu.SemaphoreType.DMA((3, NCH)),
            pltpu.SemaphoreType.DMA((4, NCH)),
            pltpu.SemaphoreType.DMA((4, NCH)),
            pltpu.SemaphoreType.DMA((NCH,)),
        ],
        compiler_params=pltpu.CompilerParams(
            collective_id=1, has_side_effects=True, vmem_limit_bytes=LIMIT
        ),
    )(got)
    return vis.reshape(2, 4 * KD, ROWS, INPUTS).astype(F32)


def solution(mesh):
    in_specs = (P("tile", "chan"), P("tile", None), P())
    out_specs = P(None, "chan", "tile", None)
    return jax.shard_map(body, mesh=mesh, in_specs=in_specs, out_specs=out_specs, check_vma=False)
```

```python
import functools
import math

import jax
import jax.numpy as jnp
import numpy as np
from jax import lax
from jax.experimental import pallas as pl
from jax.experimental.pallas import tpu as pltpu
from jax.sharding import PartitionSpec as P

CH = 1024
TAPS = 16
FFT = 2048
SPEC = 128
INPUTS = 512

NT = FFT // 128
CHAN = 8
ROWS = 32
OWN = ROWS // CHAN
SLOC = SPEC // CHAN
RC = 4
NR = NT // RC
CHUNKS = 4
MIXED = 6
KEPT = 4
PER = MIXED + KEPT
GROUP = 4 * MIXED + 2 * KEPT
STEP = 2
SUBS = PER // STEP
NSUB = CHUNKS * SUBS
AHEAD = 2
LIMIT = 62 << 20
DBG = ()

MESH = pl.DeviceIdType.MESH
F32 = jnp.float32
BF16 = jnp.bfloat16


def phase_tables():
    k = np.arange(CH, dtype=np.int64).reshape(CHAN, CHUNKS, GROUP).transpose(1, 0, 2).reshape(-1)
    fine = (k[:, None] * np.arange(128)[None, :]) % FFT * (2.0 * math.pi / FFT)
    fine = np.stack([np.cos(fine), np.sin(fine)]) / math.sqrt(CH)
    coarse = (np.arange(NT)[:, None] * np.arange(16)[None, :]) % 16 * (2.0 * math.pi / 16)
    coarse = np.stack([np.cos(coarse), np.sin(coarse)])
    coarse = np.broadcast_to(coarse[..., None], (2, NT, 16, 128))
    return fine.astype(np.float32), np.ascontiguousarray(coarse).astype(np.float32)


def place():
    tile, chan = lax.axis_index("tile"), lax.axis_index("chan")
    x_lo, z, core = tile // 8, (tile // 2) % 4, tile % 2
    return tile, chan, x_lo, z, core


def plane_tile(q, z):
    return (q // 2) * 8 + z * 2 + q % 2


def kernel(
    volt, hist, taps, fine, coarse, out,
    h8, table, pack, hpack, send, recv, ext, filt, fir, spec, out2, got, gather, obm, obk,
    hsem, s1, r1, s2, r2, sz, rz, sm, rm, sk, rk, lsem,
):
    tile, chan, x_lo, z, core = place()
    q = x_lo * 2 + core
    up, down, far = lax.rem(z + 1, 4), lax.rem(z + 3, 4), lax.rem(z + 2, 4)
    hcopy = pltpu.make_async_copy(
        hist.at[pl.ds(pl.multiple_of((chan // 2) * 8, 8), 8), :], h8, hsem
    )
    hcopy.start()

    barrier = pltpu.get_barrier_semaphore()

    @pl.loop(1, 32)
    def _(i):
        other = lax.rem(q * 8 + chan + i, 32)
        pl.semaphore_signal(
            barrier, inc=1, device_id=(plane_tile(other // 8, z), other % 8), device_id_type=MESH
        )

    for nz in (up, down):
        pl.semaphore_signal(
            barrier, inc=1, device_id=(plane_tile(q, nz), chan), device_id_type=MESH
        )

    def first(i, r):
        to = lax.rem(chan + i, CHAN)
        part = pl.ds(r * NR, NR)
        return pltpu.make_async_remote_copy(
            src_ref=send.at[to, part], dst_ref=recv.at[chan, part],
            send_sem=s1.at[r, to], recv_sem=r1.at[r, chan],
            device_id=(tile, to), device_id_type=MESH,
        )

    def first_in(i, r):
        src = lax.rem(chan + CHAN - i, CHAN)
        part = pl.ds(r * NR, NR)
        return pltpu.make_async_remote_copy(
            src_ref=send.at[src, part], dst_ref=recv.at[src, part],
            send_sem=s1.at[r, src], recv_sem=r1.at[r, src],
            device_id=(tile, src), device_id_type=MESH,
        )

    def pack_part(r):
        @pl.loop(r * NR, r * NR + NR)
        def _(nt):
            for s in range(SLOC):
                lanes = pl.ds(pl.multiple_of(s * FFT + nt * 128, 128), 128)
                pack[pl.ds(s, ROWS, stride=SLOC), :] = volt[:, lanes].astype(F32)
            for c in range(CHAN):
                send[c, nt] = pack[pl.ds(c * OWN * SLOC, OWN * SLOC), :].astype(BF16)

    def send_part(r):
        @pl.loop(1, CHAN)
        def _(i):
            first(i, r).start()

    pack_part(0)
    pl.semaphore_wait(barrier, 33)
    send_part(0)

    @pl.loop(1, RC)
    def _(r):
        pack_part(r)
        send_part(r)

    recv[chan] = send[chan]
    hcopy.wait()

    @pl.loop(0, CH // 16)
    def _(kb):
        rows = pl.ds(pl.multiple_of(kb * 16, 16), 16)
        chunk = kb // 16
        base = chunk * 512 + lax.rem(kb, 16) * 16
        rows_re = pl.ds(pl.multiple_of(base, 16), 16)
        rows_im = pl.ds(pl.multiple_of(base + 256, 16), 16)
        c2, s2_ = fine[0, rows, :], fine[1, rows, :]
        for n1 in range(NT):
            c1, s1_ = coarse[0, n1], coarse[1, n1]
            lanes = pl.ds(n1 * 128, 128)
            table[rows_re, lanes] = (c1 * c2 - s1_ * s2_).astype(BF16)
            table[rows_im, lanes] = (-(s1_ * c2 + c1 * s2_)).astype(BF16)

    odd = lax.rem(chan, 2)

    @pl.loop(0, NT)
    def _(nt):
        @pl.when(lax.rem(nt, NR) == 0)
        def _():
            @pl.loop(1, CHAN)
            def _(i):
                first_in(i, nt // NR).wait_recv()

        for j in range(TAPS - 1):
            lanes = pl.ds(pl.multiple_of(j * FFT + nt * 128, 128), 128)
            hpack[pl.ds(j + 1, 8, stride=16), :] = h8[:, lanes].astype(F32)
        for a in range(OWN):
            old = hpack[pl.ds(pl.multiple_of(odd * 64 + a * 16, 16), 16), :]
            ext[pl.ds(a * 2, 16, stride=8), :] = old
        for c in range(CHAN):
            for a in range(OWN):
                part = recv[c, nt, a * 16 : (a + 1) * 16, :].astype(F32)
                start = (16 + (c % 4) * 16) * 8 + a * 2 + c // 4
                ext[pl.ds(start, 16, stride=8), :] = part
                if c == 3:
                    ext[pl.ds(a * 2 + 1, 16, stride=8), :] = part
        lanes = pl.ds(pl.multiple_of(nt * 128, 128), 128)
        weights = [
            jnp.broadcast_to(taps[t : t + 1, lanes].astype(F32), (8, 128)) for t in range(TAPS)
        ]

        @pl.loop(0, 64, step=8)
        def _(j0):
            base = pl.multiple_of(j0 * 8, 64)
            rows = [ext[pl.ds(base + (r + 1) * 8, 8), :] for r in range(8 + TAPS - 1)]
            for j in range(8):
                total = weights[0] * rows[j]
                for t in range(1, TAPS):
                    total = total + weights[t] * rows[j + t]
                fir[pl.ds(j0 + j, 8, stride=64), :] = total * (1.0 / 16384.0)

        filt[:, lanes] = fir[...].astype(BF16)

    def second(chunk, to, to_chan, src, src_chan):
        return pltpu.make_async_remote_copy(
            src_ref=out2.at[chunk, to_chan, to], dst_ref=got.at[chunk, src, src_chan],
            send_sem=s2.at[chunk, to, to_chan], recv_sem=r2.at[chunk, src, src_chan],
            device_id=(plane_tile(to, z), to_chan), device_id_type=MESH,
        )

    def dft(chunk):
        for p in range(2):
            rows = pl.ds(pl.multiple_of(chunk * 512 + p * 256, 256), 256)
            block = lax.dot_general(
                table[rows, :], filt[...], (((1,), (1,)), ((), ())), preferred_element_type=F32
            )
            for a in range(OWN):
                spec[pl.ds(p * OWN + a, 256, stride=8), :] = block[:, a * 128 : (a + 1) * 128]
        for c in range(CHAN):
            for to in range(4):
                start = (c * GROUP + MIXED * to) * 8
                out2[chunk, c, to, 0 : MIXED * 8, :] = spec[start : start + MIXED * 8, :].astype(BF16)
                start = (c * GROUP + 4 * MIXED + KEPT * (to % 2)) * 8
                out2[chunk, c, to, MIXED * 8 : PER * 8, :] = spec[start : start + KEPT * 8, :].astype(BF16)
        got[chunk, q, chan] = out2[chunk, chan, q]

        @pl.loop(1, 32)
        def _(i):
            other = lax.rem(q * 8 + chan + i, 32)
            second(chunk, other // 8, other % 8, q, chan).start()

    def arrive(chunk):
        @pl.loop(1, 32)
        def _(i):
            other = lax.rem(q * 8 + chan + 32 - i, 32)
            second(chunk, other // 8, other % 8, other // 8, other % 8).wait_recv()

    low = lax.broadcasted_iota(jnp.int32, (8, 128), 0) < 4

    def assemble(chunk):
        @pl.loop(0, PER // 2)
        def _(kp):
            rows = pl.ds(pl.multiple_of(kp * 16, 16), 16)
            for member in range(4):
                mx, mc = member // 2, member % 2
                for half in range(2):
                    parts = [
                        got[chunk, member, half * 4 + c, rows, :].astype(F32) for c in range(4)
                    ]
                    for kk in range(2):
                        v = [part[kk * 8 : kk * 8 + 8, :] for part in parts]
                        r = [pltpu.roll(x, 4, 0) for x in v]
                        re = jnp.concatenate(
                            [jnp.where(low, v[0], r[1]), jnp.where(low, v[2], r[3])], axis=0
                        )
                        im = jnp.concatenate(
                            [jnp.where(low, r[0], v[1]), jnp.where(low, r[2], v[3])], axis=0
                        )
                        at = pl.ds(mc * 32 + half * 16, 16)
                        channel = chunk * PER + kp * 2 + kk
                        gather[channel, mx, z, at, 0:128] = re.astype(BF16)
                        gather[channel, mx, z, at, 128:256] = im.astype(BF16)

    def split(step):
        return step // SUBS, lax.rem(step, SUBS)

    def channel_of(step):
        chunk, j = split(step)
        return chunk * PER + jnp.where(lax.rem(j, 2) == 0, j, MIXED - 1 + j)

    def shift(step, owner, to, way):
        block = gather.at[pl.ds(channel_of(step), STEP), :, owner]
        return pltpu.make_async_remote_copy(
            src_ref=block, dst_ref=block, send_sem=sz.at[way, step], recv_sem=rz.at[way, step],
            device_id=(plane_tile(q, to), chan), device_id_type=MESH,
        )

    def mixed_rows(chunk, j, src):
        return out.at[:, pl.ds(chunk * GROUP + MIXED * src + j, STEP)]

    def mixed_part(chunk, j, to):
        return obm.at[to, :, pl.ds(chunk * MIXED + j, STEP)]

    def spread(chunk, j, to, src):
        at = chunk * (MIXED // 2) + j // 2
        return pltpu.make_async_remote_copy(
            src_ref=mixed_part(chunk, j, to), dst_ref=mixed_rows(chunk, j, src),
            send_sem=sm.at[to, at], recv_sem=rm.at[src, at],
            device_id=(plane_tile(to, z), chan), device_id_type=MESH,
        )

    def spread_own(chunk, j):
        return pltpu.make_async_copy(
            mixed_part(chunk, j, q), mixed_rows(chunk, j, q), lsem.at[chunk * SUBS + j]
        )

    def kept_rows(chunk, j, src):
        return out.at[:, pl.ds(chunk * GROUP + 4 * MIXED + KEPT * src + j - 1, STEP)]

    def kept_part(chunk, j, to):
        return obk.at[to, :, pl.ds(chunk * KEPT + j - 1, STEP)]

    def pair(chunk, j, src):
        at = chunk * (KEPT // 2) + j // 2
        return pltpu.make_async_remote_copy(
            src_ref=kept_part(chunk, j, 1 - core), dst_ref=kept_rows(chunk, j, src),
            send_sem=sk.at[at], recv_sem=rk.at[at],
            device_id=(plane_tile(x_lo * 2 + 1 - core, z), chan), device_id_type=MESH,
        )

    def pair_own(chunk, j):
        return pltpu.make_async_copy(
            kept_part(chunk, j, core), kept_rows(chunk, j, core), lsem.at[chunk * SUBS + j]
        )

    def correlate(mine, right):
        re, im = mine[:, :128], mine[:, 128:]
        left = jnp.concatenate([mine, jnp.concatenate([im, -re], axis=1)], axis=0)
        vis = lax.dot_general(left, right, (((1,), (1,)), ((), ())), preferred_element_type=F32)
        return (vis * (1.0 / SPEC)).astype(BF16)

    @pl.loop(0, 2)
    def _(chunk):
        dft(chunk)

    @pl.loop(0, NSUB + AHEAD + 1)
    def _(tick):
        @pl.when(tick < NSUB)
        def _():
            chunk, j = split(tick)

            @pl.when(j == 0)
            def _():
                arrive(chunk)
                assemble(chunk)

            shift(tick, z, up, 0).start()
            shift(tick, z, down, 1).start()

        @pl.when(tick < CHUNKS - 2)
        def _():
            dft(tick + 2)

        step = tick - AHEAD

        @pl.when((step >= 0) & (step < NSUB))
        def _():
            shift(step, down, up, 0).wait_recv()
            shift(step, up, down, 1).wait_recv()

            @pl.when(lax.rem(step, 2) == 0)
            def _():
                shift(step, down, up, 2).start()

            @pl.when(lax.rem(step, 2) == 1)
            def _():
                shift(step, up, down, 2).start()

        @pl.when(step > 0)
        def _():
            done = step - 1
            shift(done, far, up, 2).wait_recv()
            chunk, j = split(done)
            base = channel_of(done)

            @pl.when(lax.rem(j, 2) == 0)
            def _():
                for kk in range(STEP):
                    mine = gather[base + kk, :, z].reshape(128, 256)
                    vis = correlate(mine, gather[base + kk].reshape(INPUTS, 256))
                    for to in range(4):
                        for p in range(2):
                            first_row = p * 128 + to * 32
                            obm[to, p, chunk * MIXED + j + kk] = vis[first_row : first_row + 32, :]
                for m in (1, 2, 3):
                    spread(chunk, j, lax.rem(q + m, 4), q).start()
                spread_own(chunk, j).start()

            @pl.when(lax.rem(j, 2) == 1)
            def _():
                for kk in range(STEP):
                    mine = gather[base + kk, x_lo, z]
                    vis = correlate(mine, gather[base + kk].reshape(INPUTS, 256))
                    for to in range(2):
                        for p in range(2):
                            first_row = p * 64 + to * 32
                            obk[to, p, chunk * KEPT + j - 1 + kk] = vis[first_row : first_row + 32, :]
                pair(chunk, j, core).start()
                pair_own(chunk, j).start()

    @pl.loop(0, RC)
    def _(r):
        @pl.loop(1, CHAN)
        def _(i):
            first(i, r).wait_send()

    @pl.loop(0, CHUNKS)
    def _(chunk):
        @pl.loop(1, 32)
        def _(i):
            other = lax.rem(q * 8 + chan + i, 32)
            second(chunk, other // 8, other % 8, q, chan).wait_send()

    @pl.loop(0, NSUB)
    def _(step):
        shift(step, z, up, 0).wait_send()
        shift(step, z, down, 1).wait_send()
        shift(step, far, up, 2).wait_send()
        chunk, j = split(step)

        @pl.when(lax.rem(j, 2) == 0)
        def _():
            spread_own(chunk, j).wait()
            for m in (1, 2, 3):
                other = lax.rem(q + m, 4)
                spread(chunk, j, other, q).wait_send()
                spread(chunk, j, other, other).wait_recv()

        @pl.when(lax.rem(j, 2) == 1)
        def _():
            pair_own(chunk, j).wait()
            pair(chunk, j, core).wait_send()
            pair(chunk, j, 1 - core).wait_recv()


VM = pl.BlockSpec(memory_space=pltpu.VMEM)
ANY = pl.BlockSpec(memory_space=pl.ANY)
DMA = pltpu.SemaphoreType.DMA


def body(voltages, history, filter_taps):
    fine, coarse = (jnp.asarray(x) for x in phase_tables())
    vis = pl.pallas_call(
        kernel,
        name="correlator",
        out_shape=jax.ShapeDtypeStruct((2, CHUNKS * GROUP, ROWS, INPUTS), BF16),
        in_specs=[VM, ANY, VM, VM, VM],
        out_specs=ANY,
        scratch_shapes=[
            pltpu.VMEM((8, (TAPS - 1) * FFT), jnp.int32),
            pltpu.VMEM((2 * CH, FFT), BF16),
            pltpu.VMEM((ROWS * SLOC, 128), F32),
            pltpu.VMEM((128, 128), F32),
            pltpu.VMEM((CHAN, NT, OWN * SLOC, 128), BF16),
            pltpu.VMEM((CHAN, NT, OWN * SLOC, 128), BF16),
            pltpu.VMEM((80 * 8, 128), F32),
            pltpu.VMEM((OWN * SPEC, FFT), BF16),
            pltpu.VMEM((OWN * SPEC, 128), F32),
            pltpu.VMEM((256 * 8, 128), F32),
            pltpu.VMEM((CHUNKS, CHAN, 4, PER * 8, 128), BF16),
            pltpu.VMEM((CHUNKS, 4, CHAN, PER * 8, 128), BF16),
            pltpu.VMEM((CHUNKS * PER, 2, 4, 64, 256), BF16),
            pltpu.VMEM((4, 2, CHUNKS * MIXED, ROWS, INPUTS), BF16),
            pltpu.VMEM((2, 2, CHUNKS * KEPT, ROWS, INPUTS), BF16),
            DMA,
            DMA((RC, CHAN)),
            DMA((RC, CHAN)),
            DMA((CHUNKS, 4, CHAN)),
            DMA((CHUNKS, 4, CHAN)),
            DMA((3, NSUB)),
            DMA((3, NSUB)),
            DMA((4, CHUNKS * MIXED // 2)),
            DMA((4, CHUNKS * MIXED // 2)),
            DMA((CHUNKS * KEPT // 2,)),
            DMA((CHUNKS * KEPT // 2,)),
            DMA((NSUB,)),
        ],
        compiler_params=pltpu.CompilerParams(
            collective_id=0, has_side_effects=True, vmem_limit_bytes=LIMIT
        ),
    )(voltages, history, filter_taps, fine, coarse)
    return vis.astype(F32)


def solution(mesh):
    in_specs = (P("tile", "chan"), P("tile", None), P())
    out_specs = P(None, "chan", "tile", None)
    return jax.shard_map(body, mesh=mesh, in_specs=in_specs, out_specs=out_specs, check_vma=False)
```

```python
import functools
import math

import jax
import jax.numpy as jnp
import numpy as np
from jax import lax
from jax.experimental import pallas as pl
from jax.experimental.pallas import tpu as pltpu
from jax.sharding import PartitionSpec as P

CH = 1024
TAPS = 16
FFT = 2048
SPEC = 128
INPUTS = 512

NT = FFT // 128
CHAN = 8
ROWS = 32
OWN = ROWS // CHAN
SLOC = SPEC // CHAN
RC = 4
NR = NT // RC
CHUNKS = 4
MIXED = 6
KEPT = 4
PER = MIXED + KEPT
GROUP = 4 * MIXED + 2 * KEPT
STEP = 2
SUBS = PER // STEP
NSUB = CHUNKS * SUBS
EARLY = 3
AHEAD = 1
LAG = 1
LIMIT = 54 << 20
WIDE = 4
SLOTS = 8

MESH = pl.DeviceIdType.MESH
F32 = jnp.float32
BF16 = jnp.bfloat16


def phase_tables():
    k = np.arange(CH, dtype=np.int64).reshape(CHAN, CHUNKS, GROUP).transpose(1, 0, 2).reshape(-1)
    fine = (k[:, None] * np.arange(128)[None, :]) % FFT * (2.0 * math.pi / FFT)
    fine = np.stack([np.cos(fine), np.sin(fine)]) / math.sqrt(CH)
    coarse = (np.arange(NT)[:, None] * np.arange(16)[None, :]) % 16 * (2.0 * math.pi / 16)
    coarse = np.stack([np.cos(coarse), np.sin(coarse)])
    coarse = np.broadcast_to(coarse[..., None], (2, NT, 16, 128))
    return fine.astype(np.float32), np.ascontiguousarray(coarse).astype(np.float32)


def place():
    tile, chan = lax.axis_index("tile"), lax.axis_index("chan")
    x_lo, z, core = tile // 8, (tile // 2) % 4, tile % 2
    return tile, chan, x_lo, z, core


def plane_tile(q, z):
    return (q // 2) * 8 + z * 2 + q % 2


def kernel(
    volts, hist, taps, fines, coarses, out,
    volt, h8, fine, coarse, table, pack, hpack, send, recv, ext, filt, fir, spec, out2, got, gather, obm, obk,
    vsem, hsem, s1, r1, s2, r2, sz, rz, sm, rm, sk, rk, lsem,
):
    tile, chan, x_lo, z, core = place()
    q = x_lo * 2 + core
    up, down, far = lax.rem(z + 1, 4), lax.rem(z + 3, 4), lax.rem(z + 2, 4)
    samples = [
        pltpu.make_async_copy(volts.at[:, pl.ds(s * FFT, FFT)], volt.at[s], vsem.at[s])
        for s in range(SLOC)
    ]
    for copy in samples:
        copy.start()
    later = [
        pltpu.make_async_copy(
            hist.at[pl.ds(pl.multiple_of((chan // 2) * 8, 8), 8), :], h8, hsem.at[0]
        ),
        pltpu.make_async_copy(fines, fine, hsem.at[1]),
        pltpu.make_async_copy(coarses, coarse, hsem.at[2]),
    ]
    for copy in later:
        copy.start()

    barrier = pltpu.get_barrier_semaphore()

    @pl.loop(1, 32)
    def _(i):
        other = lax.rem(q * 8 + chan + i, 32)
        pl.semaphore_signal(
            barrier, inc=1, device_id=(plane_tile(other // 8, z), other % 8), device_id_type=MESH
        )

    for nz in (up, down):
        pl.semaphore_signal(
            barrier, inc=1, device_id=(plane_tile(q, nz), chan), device_id_type=MESH
        )

    def first(i, r):
        to = lax.rem(chan + i, CHAN)
        part = pl.ds(r * NR, NR)
        return pltpu.make_async_remote_copy(
            src_ref=send.at[to, part], dst_ref=recv.at[chan, part],
            send_sem=s1.at[r, to], recv_sem=r1.at[r, chan],
            device_id=(tile, to), device_id_type=MESH,
        )

    def first_in(i, r):
        src = lax.rem(chan + CHAN - i, CHAN)
        part = pl.ds(r * NR, NR)
        return pltpu.make_async_remote_copy(
            src_ref=send.at[src, part], dst_ref=recv.at[src, part],
            send_sem=s1.at[r, src], recv_sem=r1.at[r, src],
            device_id=(tile, src), device_id_type=MESH,
        )

    def pack_part(r):
        @pl.loop(r * NR, r * NR + NR)
        def _(nt):
            for s in range(SLOC):
                lanes = pl.ds(pl.multiple_of(nt * 128, 128), 128)
                pack[pl.ds(s, ROWS, stride=SLOC), :] = volt[s, :, lanes].astype(F32)
            for c in range(CHAN):
                send[c, nt] = pack[pl.ds(c * OWN * SLOC, OWN * SLOC), :].astype(BF16)

    def send_part(r):
        @pl.loop(1, CHAN)
        def _(i):
            first(i, r).start()

    for copy in samples:
        copy.wait()
    pack_part(0)
    pl.semaphore_wait(barrier, 33)
    send_part(0)

    @pl.loop(1, RC)
    def _(r):
        pack_part(r)
        send_part(r)

    recv[chan] = send[chan]
    for copy in later:
        copy.wait()

    @pl.loop(0, CH // 16)
    def _(kb):
        rows = pl.ds(pl.multiple_of(kb * 16, 16), 16)
        chunk = kb // 16
        base = chunk * 512 + lax.rem(kb, 16) * 16
        rows_re = pl.ds(pl.multiple_of(base, 16), 16)
        rows_im = pl.ds(pl.multiple_of(base + 256, 16), 16)
        c2, s2_ = fine[0, rows, :], fine[1, rows, :]
        for n1 in range(NT):
            c1, s1_ = coarse[0, n1], coarse[1, n1]
            lanes = pl.ds(n1 * 128, 128)
            table[rows_re, lanes] = (c1 * c2 - s1_ * s2_).astype(BF16)
            table[rows_im, lanes] = (-(s1_ * c2 + c1 * s2_)).astype(BF16)

    odd = lax.rem(chan, 2)

    @pl.loop(0, NT)
    def _(nt):
        @pl.when(lax.rem(nt, NR) == 0)
        def _():
            @pl.loop(1, CHAN)
            def _(i):
                first_in(i, nt // NR).wait_recv()

        for j in range(TAPS - 1):
            lanes = pl.ds(pl.multiple_of(j * FFT + nt * 128, 128), 128)
            hpack[pl.ds(j + 1, 8, stride=16), :] = h8[:, lanes].astype(F32)
        for a in range(OWN):
            old = hpack[pl.ds(pl.multiple_of(odd * 64 + a * 16, 16), 16), :]
            ext[pl.ds(a * 2, 16, stride=8), :] = old
        for c in range(CHAN):
            for a in range(OWN):
                part = recv[c, nt, a * 16 : (a + 1) * 16, :].astype(F32)
                start = (16 + (c % 4) * 16) * 8 + a * 2 + c // 4
                ext[pl.ds(start, 16, stride=8), :] = part
                if c == 3:
                    ext[pl.ds(a * 2 + 1, 16, stride=8), :] = part
        lanes = pl.ds(pl.multiple_of(nt * 128, 128), 128)
        weights = [
            jnp.broadcast_to(taps[t : t + 1, lanes].astype(F32), (8, 128)) for t in range(TAPS)
        ]

        @pl.loop(0, 64, step=8)
        def _(j0):
            base = pl.multiple_of(j0 * 8, 64)
            rows = [ext[pl.ds(base + (r + 1) * 8, 8), :] for r in range(8 + TAPS - 1)]
            for j in range(8):
                total = weights[0] * rows[j]
                for t in range(1, TAPS):
                    total = total + weights[t] * rows[j + t]
                fir[pl.ds(j0 + j, 8, stride=64), :] = total * (1.0 / 16384.0)

        filt[:, lanes] = fir[...].astype(BF16)

    def second(chunk, to, to_chan, src, src_chan):
        return pltpu.make_async_remote_copy(
            src_ref=out2.at[chunk, to_chan, to], dst_ref=got.at[chunk, src, src_chan],
            send_sem=s2.at[chunk, to, to_chan], recv_sem=r2.at[chunk, src, src_chan],
            device_id=(plane_tile(to, z), to_chan), device_id_type=MESH,
        )

    def dft(chunk):
        for p in range(2):
            rows = pl.ds(pl.multiple_of(chunk * 512 + p * 256, 256), 256)
            block = lax.dot_general(
                table[rows, :], filt[...], (((1,), (1,)), ((), ())), preferred_element_type=F32
            )
            for a in range(OWN):
                spec[pl.ds(p * OWN + a, 256, stride=8), :] = block[:, a * 128 : (a + 1) * 128]
        for c in range(CHAN):
            for to in range(4):
                start = (c * GROUP + MIXED * to) * 8
                out2[chunk, c, to, 0 : MIXED * 8, :] = spec[start : start + MIXED * 8, :].astype(BF16)
                start = (c * GROUP + 4 * MIXED + KEPT * (to % 2)) * 8
                out2[chunk, c, to, MIXED * 8 : PER * 8, :] = spec[start : start + KEPT * 8, :].astype(BF16)
        got[chunk, q, chan] = out2[chunk, chan, q]

        @pl.loop(1, 32)
        def _(i):
            other = lax.rem(q * 8 + chan + i, 32)
            second(chunk, other // 8, other % 8, q, chan).start()

    def arrive(chunk):
        @pl.loop(1, 32)
        def _(i):
            other = lax.rem(q * 8 + chan + 32 - i, 32)
            second(chunk, other // 8, other % 8, other // 8, other % 8).wait_recv()

    low = lax.broadcasted_iota(jnp.int32, (8, 128), 0) < 4

    def assemble(chunk):
        @pl.loop(0, PER // 2)
        def _(kp):
            rows = pl.ds(pl.multiple_of(kp * 16, 16), 16)
            for member in range(4):
                mx, mc = member // 2, member % 2
                for half in range(2):
                    parts = [
                        got[chunk, member, half * 4 + c, rows, :].astype(F32) for c in range(4)
                    ]
                    for kk in range(2):
                        v = [part[kk * 8 : kk * 8 + 8, :] for part in parts]
                        r = [pltpu.roll(x, 4, 0) for x in v]
                        re = jnp.concatenate(
                            [jnp.where(low, v[0], r[1]), jnp.where(low, v[2], r[3])], axis=0
                        )
                        im = jnp.concatenate(
                            [jnp.where(low, r[0], v[1]), jnp.where(low, r[2], v[3])], axis=0
                        )
                        at = pl.ds(mc * 32 + half * 16, 16)
                        channel = chunk * PER + kp * 2 + kk
                        gather[channel, mx, z, at, 0:128] = re.astype(BF16)
                        gather[channel, mx, z, at, 128:256] = im.astype(BF16)

    def is_kept(j):
        return (j == 1) | (j == 4)

    def mixed_at(j):
        return STEP * jnp.maximum(j - 1, 0)

    def kept_at(j):
        return 2 * (j // 4)

    def split(step):
        return step // SUBS, lax.rem(step, SUBS)

    def channel_of(step):
        chunk, j = split(step)
        return chunk * PER + jnp.where(is_kept(j), MIXED + kept_at(j), mixed_at(j))

    def shift(step, owner, to, way):
        first_one = channel_of(step) + (STEP // 2 if way == 3 else 0)
        block = gather.at[pl.ds(first_one, STEP if way < 2 else STEP // 2), :, owner]
        return pltpu.make_async_remote_copy(
            src_ref=block, dst_ref=block, send_sem=sz.at[way, step], recv_sem=rz.at[way, step],
            device_id=(plane_tile(q, to), chan), device_id_type=MESH,
        )

    def mixed_rows(chunk, j, src):
        return out.at[:, pl.ds(chunk * GROUP + MIXED * src + mixed_at(j), STEP)]

    def mixed_part(chunk, j, to):
        return obm.at[to, :, pl.ds(chunk * MIXED + mixed_at(j), STEP)]

    def spread(chunk, j, to, src):
        at = chunk * (MIXED // STEP) + mixed_at(j) // STEP
        return pltpu.make_async_remote_copy(
            src_ref=mixed_part(chunk, j, to), dst_ref=mixed_rows(chunk, j, src),
            send_sem=sm.at[to, at], recv_sem=rm.at[src, at],
            device_id=(plane_tile(to, z), chan), device_id_type=MESH,
        )

    def spread_own(chunk, j):
        return pltpu.make_async_copy(
            mixed_part(chunk, j, q), mixed_rows(chunk, j, q), lsem.at[chunk * SUBS + j]
        )

    def kept_rows(chunk, j, src):
        return out.at[:, pl.ds(chunk * GROUP + 4 * MIXED + KEPT * src + kept_at(j), STEP)]

    def kept_part(chunk, j, to):
        return obk.at[to, :, pl.ds(chunk * KEPT + kept_at(j), STEP)]

    def pair(chunk, j, src):
        at = chunk * (KEPT // STEP) + kept_at(j) // STEP
        return pltpu.make_async_remote_copy(
            src_ref=kept_part(chunk, j, 1 - core), dst_ref=kept_rows(chunk, j, src),
            send_sem=sk.at[at], recv_sem=rk.at[at],
            device_id=(plane_tile(x_lo * 2 + 1 - core, z), chan), device_id_type=MESH,
        )

    def pair_own(chunk, j):
        return pltpu.make_async_copy(
            kept_part(chunk, j, core), kept_rows(chunk, j, core), lsem.at[chunk * SUBS + j]
        )

    def correlate(mine, right):
        re, im = mine[:, :128], mine[:, 128:]
        left = jnp.concatenate([mine, jnp.concatenate([im, -re], axis=1)], axis=0)
        vis = lax.dot_general(left, right, (((1,), (1,)), ((), ())), preferred_element_type=F32)
        return (vis * (1.0 / SPEC)).astype(BF16)

    @pl.loop(0, EARLY)
    def _(chunk):
        dft(chunk)

    @pl.loop(0, NSUB + AHEAD + LAG)
    def _(tick):
        @pl.when(tick < NSUB)
        def _():
            chunk, j = split(tick)

            @pl.when(j == 0)
            def _():
                arrive(chunk)
                assemble(chunk)

            shift(tick, z, up, 0).start()
            shift(tick, z, down, 1).start()

        @pl.when(tick < CHUNKS - EARLY)
        def _():
            dft(tick + EARLY)

        step = tick - AHEAD

        @pl.when((step >= 0) & (step < NSUB))
        def _():
            shift(step, down, up, 0).wait_recv()
            shift(step, up, down, 1).wait_recv()

            shift(step, down, up, 2).start()
            shift(step, up, down, 3).start()

        @pl.when(step >= LAG)
        def _():
            done = step - LAG
            shift(done, far, up, 2).wait_recv()
            shift(done, far, down, 3).wait_recv()
            chunk, j = split(done)
            base = channel_of(done)

            @pl.when(jnp.logical_not(is_kept(j)))
            def _():
                for kk in range(STEP):
                    mine = gather[base + kk, :, z].reshape(128, 256)
                    vis = correlate(mine, gather[base + kk].reshape(INPUTS, 256))
                    for to in range(4):
                        for p in range(2):
                            first_row = p * 128 + to * 32
                            obm[to, p, chunk * MIXED + mixed_at(j) + kk] = vis[first_row : first_row + 32, :]
                for m in (1, 2, 3):
                    spread(chunk, j, lax.rem(q + m, 4), q).start()
                spread_own(chunk, j).start()

            @pl.when(is_kept(j))
            def _():
                for kk in range(STEP):
                    mine = gather[base + kk, x_lo, z]
                    vis = correlate(mine, gather[base + kk].reshape(INPUTS, 256))
                    for to in range(2):
                        for p in range(2):
                            first_row = p * 64 + to * 32
                            obk[to, p, chunk * KEPT + kept_at(j) + kk] = vis[first_row : first_row + 32, :]
                pair(chunk, j, core).start()
                pair_own(chunk, j).start()

    @pl.loop(0, RC)
    def _(r):
        @pl.loop(1, CHAN)
        def _(i):
            first(i, r).wait_send()

    @pl.loop(0, CHUNKS)
    def _(chunk):
        @pl.loop(1, 32)
        def _(i):
            other = lax.rem(q * 8 + chan + i, 32)
            second(chunk, other // 8, other % 8, q, chan).wait_send()

    @pl.loop(0, NSUB)
    def _(step):
        shift(step, z, up, 0).wait_send()
        shift(step, z, down, 1).wait_send()
        shift(step, down, up, 2).wait_send()
        shift(step, up, down, 3).wait_send()
        chunk, j = split(step)

        @pl.when(jnp.logical_not(is_kept(j)))
        def _():
            spread_own(chunk, j).wait()
            for m in (1, 2, 3):
                other = lax.rem(q + m, 4)
                spread(chunk, j, other, q).wait_send()
                spread(chunk, j, other, other).wait_recv()

        @pl.when(is_kept(j))
        def _():
            pair_own(chunk, j).wait()
            pair(chunk, j, core).wait_send()
            pair(chunk, j, 1 - core).wait_recv()


def widen(vis, out, wide, sem):
    per_part = CHUNKS * GROUP // WIDE

    def store(block):
        slot = lax.rem(block, SLOTS)
        return pltpu.make_async_copy(
            wide.at[slot],
            out.at[block // per_part, pl.ds(lax.rem(block, per_part) * WIDE, WIDE)],
            sem.at[slot],
        )

    @pl.loop(0, 2 * per_part)
    def _(block):
        @pl.when(block >= SLOTS)
        def _():
            store(block - SLOTS).wait()

        rows = pl.ds(lax.rem(block, per_part) * WIDE, WIDE)
        wide[lax.rem(block, SLOTS)] = vis[block // per_part, rows].astype(F32)
        store(block).start()

    @pl.loop(2 * per_part - SLOTS, 2 * per_part)
    def _(block):
        store(block).wait()


VM = pl.BlockSpec(memory_space=pltpu.VMEM)
ANY = pl.BlockSpec(memory_space=pl.ANY)
DMA = pltpu.SemaphoreType.DMA


def body(voltages, history, filter_taps):
    fine, coarse = (jnp.asarray(x) for x in phase_tables())
    vis = pl.pallas_call(
        kernel,
        name="correlator",
        out_shape=pltpu.VMEM((2, CHUNKS * GROUP, ROWS, INPUTS), BF16),
        in_specs=[ANY, ANY, VM, ANY, ANY],
        out_specs=VM,
        scratch_shapes=[
            pltpu.VMEM((SLOC, ROWS, FFT), jnp.int32),
            pltpu.VMEM((8, (TAPS - 1) * FFT), jnp.int32),
            pltpu.VMEM((2, CH, 128), F32),
            pltpu.VMEM((2, NT, 16, 128), F32),
            pltpu.VMEM((2 * CH, FFT), BF16),
            pltpu.VMEM((ROWS * SLOC, 128), F32),
            pltpu.VMEM((128, 128), F32),
            pltpu.VMEM((CHAN, NT, OWN * SLOC, 128), BF16),
            pltpu.VMEM((CHAN, NT, OWN * SLOC, 128), BF16),
            pltpu.VMEM((80 * 8, 128), F32),
            pltpu.VMEM((OWN * SPEC, FFT), BF16),
            pltpu.VMEM((OWN * SPEC, 128), F32),
            pltpu.VMEM((256 * 8, 128), F32),
            pltpu.VMEM((CHUNKS, CHAN, 4, PER * 8, 128), BF16),
            pltpu.VMEM((CHUNKS, 4, CHAN, PER * 8, 128), BF16),
            pltpu.VMEM((CHUNKS * PER, 2, 4, 64, 256), BF16),
            pltpu.VMEM((4, 2, CHUNKS * MIXED, ROWS, INPUTS), BF16),
            pltpu.VMEM((2, 2, CHUNKS * KEPT, ROWS, INPUTS), BF16),
            DMA((SLOC,)),
            DMA((3,)),
            DMA((RC, CHAN)),
            DMA((RC, CHAN)),
            DMA((CHUNKS, 4, CHAN)),
            DMA((CHUNKS, 4, CHAN)),
            DMA((4, NSUB)),
            DMA((4, NSUB)),
            DMA((4, CHUNKS * MIXED // 2)),
            DMA((4, CHUNKS * MIXED // 2)),
            DMA((CHUNKS * KEPT // 2,)),
            DMA((CHUNKS * KEPT // 2,)),
            DMA((NSUB,)),
        ],
        compiler_params=pltpu.CompilerParams(
            collective_id=0, has_side_effects=True, vmem_limit_bytes=LIMIT
        ),
    )(voltages, history, filter_taps, fine, coarse)
    return pl.pallas_call(
        widen,
        name="widen",
        out_shape=jax.ShapeDtypeStruct((2, CHUNKS * GROUP, ROWS, INPUTS), F32),
        in_specs=[VM],
        out_specs=ANY,
        scratch_shapes=[pltpu.VMEM((SLOTS, WIDE, ROWS, INPUTS), F32), DMA((SLOTS,))],
        compiler_params=pltpu.CompilerParams(vmem_limit_bytes=32 << 20),
    )(vis)


def solution(mesh):
    in_specs = (P("tile", "chan"), P("tile", None), P())
    out_specs = P(None, "chan", "tile", None)
    return jax.shard_map(body, mesh=mesh, in_specs=in_specs, out_specs=out_specs, check_vma=False)
```

```python
import functools
import math

import jax
import jax.numpy as jnp
import numpy as np
from jax import lax
from jax.experimental import pallas as pl
from jax.experimental.pallas import tpu as pltpu
from jax.sharding import PartitionSpec as P

CH = 1024
TAPS = 16
FFT = 2048
SPEC = 128
INPUTS = 512

NT = FFT // 128
CHAN = 8
ROWS = 32
OWN = ROWS // CHAN
SLOC = SPEC // CHAN
RC = 8
NR = NT // RC
CHUNKS = 4
MIXED = 6
KEPT = 4
PER = MIXED + KEPT
GROUP = 4 * MIXED + 2 * KEPT
STEP = 2
SUBS = PER // STEP
NSUB = CHUNKS * SUBS
EARLY = 1
GAP = 3
AHEAD = 1
LAG = 1
LIMIT = 54 << 20
WIDE = 4
SLOTS = 8

MESH = pl.DeviceIdType.MESH
F32 = jnp.float32
BF16 = jnp.bfloat16


def phase_tables():
    k = np.arange(CH, dtype=np.int64).reshape(CHAN, CHUNKS, GROUP).transpose(1, 0, 2).reshape(-1)
    fine = (k[:, None] * np.arange(128)[None, :]) % FFT * (2.0 * math.pi / FFT)
    fine = np.stack([np.cos(fine), np.sin(fine)]) / math.sqrt(CH)
    coarse = (np.arange(NT)[:, None] * np.arange(16)[None, :]) % 16 * (2.0 * math.pi / 16)
    coarse = np.stack([np.cos(coarse), np.sin(coarse)])
    coarse = np.broadcast_to(coarse[..., None], (2, NT, 16, 128))
    return fine.astype(np.float32), np.ascontiguousarray(coarse).astype(np.float32)


def place():
    tile, chan = lax.axis_index("tile"), lax.axis_index("chan")
    x_lo, z, core = tile // 8, (tile // 2) % 4, tile % 2
    return tile, chan, x_lo, z, core


def plane_tile(q, z):
    return (q // 2) * 8 + z * 2 + q % 2


def kernel(
    volts, hist, taps, fines, coarses, out,
    volt, h8, fine, coarse, table, pack, hpack, send, recv, ext, filt, fir, spec, out2, got, gather, obm, obk,
    vsem, hsem, s1, r1, s2, r2, sz, rz, sm, rm, sk, rk, lsem,
):
    tile, chan, x_lo, z, core = place()
    q = x_lo * 2 + core
    up, down, far = lax.rem(z + 1, 4), lax.rem(z + 3, 4), lax.rem(z + 2, 4)
    samples = [
        pltpu.make_async_copy(volts.at[:, pl.ds(s * FFT, FFT)], volt.at[s], vsem.at[s])
        for s in range(SLOC)
    ]
    for copy in samples:
        copy.start()
    later = [
        pltpu.make_async_copy(
            hist.at[pl.ds(pl.multiple_of((chan // 2) * 8, 8), 8), :], h8, hsem.at[0]
        ),
        pltpu.make_async_copy(fines, fine, hsem.at[1]),
        pltpu.make_async_copy(coarses, coarse, hsem.at[2]),
    ]
    for copy in later:
        copy.start()

    barrier = pltpu.get_barrier_semaphore()

    @pl.loop(1, 32)
    def _(i):
        other = lax.rem(q * 8 + chan + i, 32)
        pl.semaphore_signal(
            barrier, inc=1, device_id=(plane_tile(other // 8, z), other % 8), device_id_type=MESH
        )

    for nz in (up, down):
        pl.semaphore_signal(
            barrier, inc=1, device_id=(plane_tile(q, nz), chan), device_id_type=MESH
        )

    def first(i, r):
        to = lax.rem(chan + i, CHAN)
        part = pl.ds(r * NR, NR)
        return pltpu.make_async_remote_copy(
            src_ref=send.at[to, part], dst_ref=recv.at[chan, part],
            send_sem=s1.at[r, to], recv_sem=r1.at[r, chan],
            device_id=(tile, to), device_id_type=MESH,
        )

    def first_in(i, r):
        src = lax.rem(chan + CHAN - i, CHAN)
        part = pl.ds(r * NR, NR)
        return pltpu.make_async_remote_copy(
            src_ref=send.at[src, part], dst_ref=recv.at[src, part],
            send_sem=s1.at[r, src], recv_sem=r1.at[r, src],
            device_id=(tile, src), device_id_type=MESH,
        )

    def pack_part(r):
        @pl.loop(r * NR, r * NR + NR)
        def _(nt):
            for s in range(SLOC):
                lanes = pl.ds(pl.multiple_of(nt * 128, 128), 128)
                pack[pl.ds(s, ROWS, stride=SLOC), :] = volt[s, :, lanes].astype(F32)
            for c in range(CHAN):
                send[c, nt] = pack[pl.ds(c * OWN * SLOC, OWN * SLOC), :].astype(BF16)

    def send_part(r):
        @pl.loop(1, CHAN)
        def _(i):
            first(i, r).start()

    for copy in samples:
        copy.wait()
    pack_part(0)
    pl.semaphore_wait(barrier, 33)
    send_part(0)

    @pl.loop(1, RC)
    def _(r):
        pack_part(r)
        send_part(r)

    recv[chan] = send[chan]
    for copy in later:
        copy.wait()

    @pl.loop(0, CH // 16)
    def _(kb):
        rows = pl.ds(pl.multiple_of(kb * 16, 16), 16)
        chunk = kb // 16
        base = chunk * 512 + lax.rem(kb, 16) * 16
        rows_re = pl.ds(pl.multiple_of(base, 16), 16)
        rows_im = pl.ds(pl.multiple_of(base + 256, 16), 16)
        c2, s2_ = fine[0, rows, :], fine[1, rows, :]
        for n1 in range(NT):
            c1, s1_ = coarse[0, n1], coarse[1, n1]
            lanes = pl.ds(n1 * 128, 128)
            table[rows_re, lanes] = (c1 * c2 - s1_ * s2_).astype(BF16)
            table[rows_im, lanes] = (-(s1_ * c2 + c1 * s2_)).astype(BF16)

    odd = lax.rem(chan, 2)

    @pl.loop(0, NT)
    def _(nt):
        @pl.when(lax.rem(nt, NR) == 0)
        def _():
            @pl.loop(1, CHAN)
            def _(i):
                first_in(i, nt // NR).wait_recv()

        for j in range(TAPS - 1):
            lanes = pl.ds(pl.multiple_of(j * FFT + nt * 128, 128), 128)
            hpack[pl.ds(j + 1, 8, stride=16), :] = h8[:, lanes].astype(F32)
        for a in range(OWN):
            old = hpack[pl.ds(pl.multiple_of(odd * 64 + a * 16, 16), 16), :]
            ext[pl.ds(a * 2, 16, stride=8), :] = old
        for c in range(CHAN):
            for a in range(OWN):
                part = recv[c, nt, a * 16 : (a + 1) * 16, :].astype(F32)
                start = (16 + (c % 4) * 16) * 8 + a * 2 + c // 4
                ext[pl.ds(start, 16, stride=8), :] = part
                if c == 3:
                    ext[pl.ds(a * 2 + 1, 16, stride=8), :] = part
        lanes = pl.ds(pl.multiple_of(nt * 128, 128), 128)
        weights = [
            jnp.broadcast_to(taps[t : t + 1, lanes].astype(F32), (8, 128)) for t in range(TAPS)
        ]

        @pl.loop(0, 64, step=8)
        def _(j0):
            base = pl.multiple_of(j0 * 8, 64)
            rows = [ext[pl.ds(base + (r + 1) * 8, 8), :] for r in range(8 + TAPS - 1)]
            for j in range(8):
                total = weights[0] * rows[j]
                for t in range(1, TAPS):
                    total = total + weights[t] * rows[j + t]
                fir[pl.ds(j0 + j, 8, stride=64), :] = total * (1.0 / 16384.0)

        filt[:, lanes] = fir[...].astype(BF16)

    def second(chunk, to, to_chan, src, src_chan):
        return pltpu.make_async_remote_copy(
            src_ref=out2.at[chunk, to_chan, to], dst_ref=got.at[chunk, src, src_chan],
            send_sem=s2.at[chunk, to, to_chan], recv_sem=r2.at[chunk, src, src_chan],
            device_id=(plane_tile(to, z), to_chan), device_id_type=MESH,
        )

    def dft(chunk):
        for p in range(2):
            rows = pl.ds(pl.multiple_of(chunk * 512 + p * 256, 256), 256)
            block = lax.dot_general(
                table[rows, :], filt[...], (((1,), (1,)), ((), ())), preferred_element_type=F32
            )
            for a in range(OWN):
                spec[pl.ds(p * OWN + a, 256, stride=8), :] = block[:, a * 128 : (a + 1) * 128]
        for c in range(CHAN):
            for to in range(4):
                start = (c * GROUP + MIXED * to) * 8
                out2[chunk, c, to, 0 : MIXED * 8, :] = spec[start : start + MIXED * 8, :].astype(BF16)
                start = (c * GROUP + 4 * MIXED + KEPT * (to % 2)) * 8
                out2[chunk, c, to, MIXED * 8 : PER * 8, :] = spec[start : start + KEPT * 8, :].astype(BF16)
        got[chunk, q, chan] = out2[chunk, chan, q]

        @pl.loop(1, 32)
        def _(i):
            other = lax.rem(q * 8 + chan + i, 32)
            second(chunk, other // 8, other % 8, q, chan).start()

    def arrive(chunk):
        @pl.loop(1, 32)
        def _(i):
            other = lax.rem(q * 8 + chan + 32 - i, 32)
            second(chunk, other // 8, other % 8, other // 8, other % 8).wait_recv()

    low = lax.broadcasted_iota(jnp.int32, (8, 128), 0) < 4

    def assemble(chunk):
        @pl.loop(0, PER // 2)
        def _(kp):
            rows = pl.ds(pl.multiple_of(kp * 16, 16), 16)
            for member in range(4):
                mx, mc = member // 2, member % 2
                for half in range(2):
                    parts = [
                        got[chunk, member, half * 4 + c, rows, :].astype(F32) for c in range(4)
                    ]
                    for kk in range(2):
                        v = [part[kk * 8 : kk * 8 + 8, :] for part in parts]
                        r = [pltpu.roll(x, 4, 0) for x in v]
                        re = jnp.concatenate(
                            [jnp.where(low, v[0], r[1]), jnp.where(low, v[2], r[3])], axis=0
                        )
                        im = jnp.concatenate(
                            [jnp.where(low, r[0], v[1]), jnp.where(low, r[2], v[3])], axis=0
                        )
                        at = pl.ds(mc * 32 + half * 16, 16)
                        channel = chunk * PER + kp * 2 + kk
                        gather[channel, mx, z, at, 0:128] = re.astype(BF16)
                        gather[channel, mx, z, at, 128:256] = im.astype(BF16)

    def is_kept(j):
        return (j == 1) | (j == 4)

    def mixed_at(j):
        return STEP * jnp.maximum(j - 1, 0)

    def kept_at(j):
        return 2 * (j // 4)

    def split(step):
        return step // SUBS, lax.rem(step, SUBS)

    def channel_of(step):
        chunk, j = split(step)
        return chunk * PER + jnp.where(is_kept(j), MIXED + kept_at(j), mixed_at(j))

    def shift(step, owner, to, way):
        first_one = channel_of(step) + (STEP // 2 if way == 3 else 0)
        block = gather.at[pl.ds(first_one, STEP if way < 2 else STEP // 2), :, owner]
        return pltpu.make_async_remote_copy(
            src_ref=block, dst_ref=block, send_sem=sz.at[way, step], recv_sem=rz.at[way, step],
            device_id=(plane_tile(q, to), chan), device_id_type=MESH,
        )

    def mixed_rows(chunk, j, src):
        return out.at[:, pl.ds(chunk * GROUP + MIXED * src + mixed_at(j), STEP)]

    def mixed_part(chunk, j, to):
        return obm.at[to, :, pl.ds(chunk * MIXED + mixed_at(j), STEP)]

    def spread(chunk, j, to, src):
        at = chunk * (MIXED // STEP) + mixed_at(j) // STEP
        return pltpu.make_async_remote_copy(
            src_ref=mixed_part(chunk, j, to), dst_ref=mixed_rows(chunk, j, src),
            send_sem=sm.at[to, at], recv_sem=rm.at[src, at],
            device_id=(plane_tile(to, z), chan), device_id_type=MESH,
        )

    def spread_own(chunk, j):
        return pltpu.make_async_copy(
            mixed_part(chunk, j, q), mixed_rows(chunk, j, q), lsem.at[chunk * SUBS + j]
        )

    def kept_rows(chunk, j, src):
        return out.at[:, pl.ds(chunk * GROUP + 4 * MIXED + KEPT * src + kept_at(j), STEP)]

    def kept_part(chunk, j, to):
        return obk.at[to, :, pl.ds(chunk * KEPT + kept_at(j), STEP)]

    def pair(chunk, j, src):
        at = chunk * (KEPT // STEP) + kept_at(j) // STEP
        return pltpu.make_async_remote_copy(
            src_ref=kept_part(chunk, j, 1 - core), dst_ref=kept_rows(chunk, j, src),
            send_sem=sk.at[at], recv_sem=rk.at[at],
            device_id=(plane_tile(x_lo * 2 + 1 - core, z), chan), device_id_type=MESH,
        )

    def pair_own(chunk, j):
        return pltpu.make_async_copy(
            kept_part(chunk, j, core), kept_rows(chunk, j, core), lsem.at[chunk * SUBS + j]
        )

    def correlate(mine, right):
        re, im = mine[:, :128], mine[:, 128:]
        left = jnp.concatenate([mine, jnp.concatenate([im, -re], axis=1)], axis=0)
        vis = lax.dot_general(left, right, (((1,), (1,)), ((), ())), preferred_element_type=F32)
        return (vis * (1.0 / SPEC)).astype(BF16)

    @pl.loop(0, EARLY)
    def _(chunk):
        dft(chunk)

    @pl.loop(0, NSUB + AHEAD + LAG)
    def _(tick):
        @pl.when(tick < NSUB)
        def _():
            chunk, j = split(tick)

            @pl.when(j == 0)
            def _():
                arrive(chunk)
                assemble(chunk)

            shift(tick, z, up, 0).start()
            shift(tick, z, down, 1).start()

        @pl.when((lax.rem(tick, GAP) == 0) & (tick // GAP < CHUNKS - EARLY))
        def _():
            dft(tick // GAP + EARLY)

        step = tick - AHEAD

        @pl.when((step >= 0) & (step < NSUB))
        def _():
            shift(step, down, up, 0).wait_recv()
            shift(step, up, down, 1).wait_recv()

            shift(step, down, up, 2).start()
            shift(step, up, down, 3).start()

        @pl.when(step >= LAG)
        def _():
            done = step - LAG
            shift(done, far, up, 2).wait_recv()
            shift(done, far, down, 3).wait_recv()
            chunk, j = split(done)
            base = channel_of(done)

            @pl.when(jnp.logical_not(is_kept(j)))
            def _():
                for kk in range(STEP):
                    mine = gather[base + kk, :, z].reshape(128, 256)
                    vis = correlate(mine, gather[base + kk].reshape(INPUTS, 256))
                    for to in range(4):
                        for p in range(2):
                            first_row = p * 128 + to * 32
                            obm[to, p, chunk * MIXED + mixed_at(j) + kk] = vis[first_row : first_row + 32, :]
                for m in (1, 2, 3):
                    spread(chunk, j, lax.rem(q + m, 4), q).start()
                spread_own(chunk, j).start()

            @pl.when(is_kept(j))
            def _():
                for kk in range(STEP):
                    mine = gather[base + kk, x_lo, z]
                    vis = correlate(mine, gather[base + kk].reshape(INPUTS, 256))
                    for to in range(2):
                        for p in range(2):
                            first_row = p * 64 + to * 32
                            obk[to, p, chunk * KEPT + kept_at(j) + kk] = vis[first_row : first_row + 32, :]
                pair(chunk, j, core).start()
                pair_own(chunk, j).start()

    @pl.loop(0, RC)
    def _(r):
        @pl.loop(1, CHAN)
        def _(i):
            first(i, r).wait_send()

    @pl.loop(0, CHUNKS)
    def _(chunk):
        @pl.loop(1, 32)
        def _(i):
            other = lax.rem(q * 8 + chan + i, 32)
            second(chunk, other // 8, other % 8, q, chan).wait_send()

    @pl.loop(0, NSUB)
    def _(step):
        shift(step, z, up, 0).wait_send()
        shift(step, z, down, 1).wait_send()
        shift(step, down, up, 2).wait_send()
        shift(step, up, down, 3).wait_send()
        chunk, j = split(step)

        @pl.when(jnp.logical_not(is_kept(j)))
        def _():
            spread_own(chunk, j).wait()
            for m in (1, 2, 3):
                other = lax.rem(q + m, 4)
                spread(chunk, j, other, q).wait_send()
                spread(chunk, j, other, other).wait_recv()

        @pl.when(is_kept(j))
        def _():
            pair_own(chunk, j).wait()
            pair(chunk, j, core).wait_send()
            pair(chunk, j, 1 - core).wait_recv()


def widen(vis, out, wide, sem):
    per_part = CHUNKS * GROUP // WIDE

    def store(block):
        slot = lax.rem(block, SLOTS)
        return pltpu.make_async_copy(
            wide.at[slot],
            out.at[block // per_part, pl.ds(lax.rem(block, per_part) * WIDE, WIDE)],
            sem.at[slot],
        )

    @pl.loop(0, 2 * per_part)
    def _(block):
        @pl.when(block >= SLOTS)
        def _():
            store(block - SLOTS).wait()

        rows = pl.ds(lax.rem(block, per_part) * WIDE, WIDE)
        wide[lax.rem(block, SLOTS)] = vis[block // per_part, rows].astype(F32)
        store(block).start()

    @pl.loop(2 * per_part - SLOTS, 2 * per_part)
    def _(block):
        store(block).wait()


VM = pl.BlockSpec(memory_space=pltpu.VMEM)
ANY = pl.BlockSpec(memory_space=pl.ANY)
DMA = pltpu.SemaphoreType.DMA


def body(voltages, history, filter_taps):
    fine, coarse = (jnp.asarray(x) for x in phase_tables())
    vis = pl.pallas_call(
        kernel,
        name="correlator",
        out_shape=pltpu.VMEM((2, CHUNKS * GROUP, ROWS, INPUTS), BF16),
        in_specs=[ANY, ANY, VM, ANY, ANY],
        out_specs=VM,
        scratch_shapes=[
            pltpu.VMEM((SLOC, ROWS, FFT), jnp.int32),
            pltpu.VMEM((8, (TAPS - 1) * FFT), jnp.int32),
            pltpu.VMEM((2, CH, 128), F32),
            pltpu.VMEM((2, NT, 16, 128), F32),
            pltpu.VMEM((2 * CH, FFT), BF16),
            pltpu.VMEM((ROWS * SLOC, 128), F32),
            pltpu.VMEM((128, 128), F32),
            pltpu.VMEM((CHAN, NT, OWN * SLOC, 128), BF16),
            pltpu.VMEM((CHAN, NT, OWN * SLOC, 128), BF16),
            pltpu.VMEM((80 * 8, 128), F32),
            pltpu.VMEM((OWN * SPEC, FFT), BF16),
            pltpu.VMEM((OWN * SPEC, 128), F32),
            pltpu.VMEM((256 * 8, 128), F32),
            pltpu.VMEM((CHUNKS, CHAN, 4, PER * 8, 128), BF16),
            pltpu.VMEM((CHUNKS, 4, CHAN, PER * 8, 128), BF16),
            pltpu.VMEM((CHUNKS * PER, 2, 4, 64, 256), BF16),
            pltpu.VMEM((4, 2, CHUNKS * MIXED, ROWS, INPUTS), BF16),
            pltpu.VMEM((2, 2, CHUNKS * KEPT, ROWS, INPUTS), BF16),
            DMA((SLOC,)),
            DMA((3,)),
            DMA((RC, CHAN)),
            DMA((RC, CHAN)),
            DMA((CHUNKS, 4, CHAN)),
            DMA((CHUNKS, 4, CHAN)),
            DMA((4, NSUB)),
            DMA((4, NSUB)),
            DMA((4, CHUNKS * MIXED // 2)),
            DMA((4, CHUNKS * MIXED // 2)),
            DMA((CHUNKS * KEPT // 2,)),
            DMA((CHUNKS * KEPT // 2,)),
            DMA((NSUB,)),
        ],
        compiler_params=pltpu.CompilerParams(
            collective_id=0, has_side_effects=True, vmem_limit_bytes=LIMIT
        ),
    )(voltages, history, filter_taps, fine, coarse)
    return pl.pallas_call(
        widen,
        name="widen",
        out_shape=jax.ShapeDtypeStruct((2, CHUNKS * GROUP, ROWS, INPUTS), F32),
        in_specs=[VM],
        out_specs=ANY,
        scratch_shapes=[pltpu.VMEM((SLOTS, WIDE, ROWS, INPUTS), F32), DMA((SLOTS,))],
        compiler_params=pltpu.CompilerParams(vmem_limit_bytes=32 << 20),
    )(vis)


def solution(mesh):
    in_specs = (P("tile", "chan"), P("tile", None), P())
    out_specs = P(None, "chan", "tile", None)
    return jax.shard_map(body, mesh=mesh, in_specs=in_specs, out_specs=out_specs, check_vma=False)
```

```python
import functools
import math

import jax
import jax.numpy as jnp
import numpy as np
from jax import lax
from jax.experimental import pallas as pl
from jax.experimental.pallas import tpu as pltpu
from jax.sharding import PartitionSpec as P

CH = 1024
TAPS = 16
FFT = 2048
SPEC = 128
INPUTS = 512

NT = FFT // 128
CHAN = 8
ROWS = 32
OWN = ROWS // CHAN
SLOC = SPEC // CHAN
RC = 16
NR = NT // RC
CHUNKS = 4
MIXED = 6
KEPT = 4
PER = MIXED + KEPT
GROUP = 4 * MIXED + 2 * KEPT
STEP = 2
SUBS = PER // STEP
NSUB = CHUNKS * SUBS
EARLY = 1
GAP = 3
AHEAD = 1
LAG = 1
LIMIT = 54 << 20
WIDE = 4
SLOTS = 8

MESH = pl.DeviceIdType.MESH
F32 = jnp.float32
BF16 = jnp.bfloat16


def phase_tables():
    k = np.arange(CH, dtype=np.int64).reshape(CHAN, CHUNKS, GROUP).transpose(1, 0, 2).reshape(-1)
    fine = (k[:, None] * np.arange(128)[None, :]) % FFT * (2.0 * math.pi / FFT)
    fine = np.stack([np.cos(fine), np.sin(fine)]) / math.sqrt(CH)
    coarse = (np.arange(NT)[:, None] * np.arange(16)[None, :]) % 16 * (2.0 * math.pi / 16)
    coarse = np.stack([np.cos(coarse), np.sin(coarse)])
    coarse = np.broadcast_to(coarse[..., None], (2, NT, 16, 128))
    return fine.astype(np.float32), np.ascontiguousarray(coarse).astype(np.float32)


def place():
    tile, chan = lax.axis_index("tile"), lax.axis_index("chan")
    x_lo, z, core = tile // 8, (tile // 2) % 4, tile % 2
    return tile, chan, x_lo, z, core


def plane_tile(q, z):
    return (q // 2) * 8 + z * 2 + q % 2


def kernel(
    volts, hist, taps, fines, coarses, out,
    volt, h8, fine, coarse, table, pack, hpack, send, recv, ext, filt, fir, spec, out2, got, gather, obm, obk,
    vsem, hsem, s1, r1, s2, r2, sz, rz, sm, rm, sk, rk, lsem,
):
    tile, chan, x_lo, z, core = place()
    q = x_lo * 2 + core
    up, down, far = lax.rem(z + 1, 4), lax.rem(z + 3, 4), lax.rem(z + 2, 4)
    samples = [
        pltpu.make_async_copy(volts.at[:, pl.ds(s * FFT, FFT)], volt.at[s], vsem.at[s])
        for s in range(SLOC)
    ]
    for copy in samples:
        copy.start()
    later = [
        pltpu.make_async_copy(
            hist.at[pl.ds(pl.multiple_of((chan // 2) * 8, 8), 8), :], h8, hsem.at[0]
        ),
        pltpu.make_async_copy(fines, fine, hsem.at[1]),
        pltpu.make_async_copy(coarses, coarse, hsem.at[2]),
    ]
    for copy in later:
        copy.start()

    barrier = pltpu.get_barrier_semaphore()

    @pl.loop(1, 32)
    def _(i):
        other = lax.rem(q * 8 + chan + i, 32)
        pl.semaphore_signal(
            barrier, inc=1, device_id=(plane_tile(other // 8, z), other % 8), device_id_type=MESH
        )

    for nz in (up, down):
        pl.semaphore_signal(
            barrier, inc=1, device_id=(plane_tile(q, nz), chan), device_id_type=MESH
        )

    def first(i, r):
        to = lax.rem(chan + i, CHAN)
        part = pl.ds(r * NR, NR)
        return pltpu.make_async_remote_copy(
            src_ref=send.at[to, part], dst_ref=recv.at[chan, part],
            send_sem=s1.at[r, to], recv_sem=r1.at[r, chan],
            device_id=(tile, to), device_id_type=MESH,
        )

    def first_in(i, r):
        src = lax.rem(chan + CHAN - i, CHAN)
        part = pl.ds(r * NR, NR)
        return pltpu.make_async_remote_copy(
            src_ref=send.at[src, part], dst_ref=recv.at[src, part],
            send_sem=s1.at[r, src], recv_sem=r1.at[r, src],
            device_id=(tile, src), device_id_type=MESH,
        )

    def pack_part(r):
        @pl.loop(r * NR, r * NR + NR)
        def _(nt):
            for s in range(SLOC):
                lanes = pl.ds(pl.multiple_of(nt * 128, 128), 128)
                pack[pl.ds(s, ROWS, stride=SLOC), :] = volt[s, :, lanes].astype(F32)
            for c in range(CHAN):
                send[c, nt] = pack[pl.ds(c * OWN * SLOC, OWN * SLOC), :].astype(BF16)

    def send_part(r):
        @pl.loop(1, CHAN)
        def _(i):
            first(i, r).start()

    for copy in samples:
        copy.wait()
    pack_part(0)
    pl.semaphore_wait(barrier, 33)
    send_part(0)

    @pl.loop(1, RC)
    def _(r):
        pack_part(r)
        send_part(r)

    recv[chan] = send[chan]
    for copy in later:
        copy.wait()

    @pl.loop(0, CH // 16)
    def _(kb):
        rows = pl.ds(pl.multiple_of(kb * 16, 16), 16)
        chunk = kb // 16
        base = chunk * 512 + lax.rem(kb, 16) * 16
        rows_re = pl.ds(pl.multiple_of(base, 16), 16)
        rows_im = pl.ds(pl.multiple_of(base + 256, 16), 16)
        c2, s2_ = fine[0, rows, :], fine[1, rows, :]
        for n1 in range(NT):
            c1, s1_ = coarse[0, n1], coarse[1, n1]
            lanes = pl.ds(n1 * 128, 128)
            table[rows_re, lanes] = (c1 * c2 - s1_ * s2_).astype(BF16)
            table[rows_im, lanes] = (-(s1_ * c2 + c1 * s2_)).astype(BF16)

    odd = lax.rem(chan, 2)

    @pl.loop(0, NT)
    def _(nt):
        @pl.when(lax.rem(nt, NR) == 0)
        def _():
            @pl.loop(1, CHAN)
            def _(i):
                first_in(i, nt // NR).wait_recv()

        for j in range(TAPS - 1):
            lanes = pl.ds(pl.multiple_of(j * FFT + nt * 128, 128), 128)
            hpack[pl.ds(j + 1, 8, stride=16), :] = h8[:, lanes].astype(F32)
        for a in range(OWN):
            old = hpack[pl.ds(pl.multiple_of(odd * 64 + a * 16, 16), 16), :]
            ext[pl.ds(a * 2, 16, stride=8), :] = old
        for c in range(CHAN):
            for a in range(OWN):
                part = recv[c, nt, a * 16 : (a + 1) * 16, :].astype(F32)
                start = (16 + (c % 4) * 16) * 8 + a * 2 + c // 4
                ext[pl.ds(start, 16, stride=8), :] = part
                if c == 3:
                    ext[pl.ds(a * 2 + 1, 16, stride=8), :] = part
        lanes = pl.ds(pl.multiple_of(nt * 128, 128), 128)
        weights = [
            jnp.broadcast_to(taps[t : t + 1, lanes].astype(F32), (8, 128)) for t in range(TAPS)
        ]

        @pl.loop(0, 64, step=8)
        def _(j0):
            base = pl.multiple_of(j0 * 8, 64)
            rows = [ext[pl.ds(base + (r + 1) * 8, 8), :] for r in range(8 + TAPS - 1)]
            for j in range(8):
                total = weights[0] * rows[j]
                for t in range(1, TAPS):
                    total = total + weights[t] * rows[j + t]
                fir[pl.ds(j0 + j, 8, stride=64), :] = total * (1.0 / 16384.0)

        filt[:, lanes] = fir[...].astype(BF16)

    def second(chunk, to, to_chan, src, src_chan):
        return pltpu.make_async_remote_copy(
            src_ref=out2.at[chunk, to_chan, to], dst_ref=got.at[chunk, src, src_chan],
            send_sem=s2.at[chunk, to, to_chan], recv_sem=r2.at[chunk, src, src_chan],
            device_id=(plane_tile(to, z), to_chan), device_id_type=MESH,
        )

    def dft(chunk):
        for p in range(2):
            rows = pl.ds(pl.multiple_of(chunk * 512 + p * 256, 256), 256)
            block = lax.dot_general(
                table[rows, :], filt[...], (((1,), (1,)), ((), ())), preferred_element_type=F32
            )
            for a in range(OWN):
                spec[pl.ds(p * OWN + a, 256, stride=8), :] = block[:, a * 128 : (a + 1) * 128]
        for c in range(CHAN):
            for to in range(4):
                start = (c * GROUP + MIXED * to) * 8
                out2[chunk, c, to, 0 : MIXED * 8, :] = spec[start : start + MIXED * 8, :].astype(BF16)
                start = (c * GROUP + 4 * MIXED + KEPT * (to % 2)) * 8
                out2[chunk, c, to, MIXED * 8 : PER * 8, :] = spec[start : start + KEPT * 8, :].astype(BF16)
        got[chunk, q, chan] = out2[chunk, chan, q]

        @pl.loop(1, 32)
        def _(i):
            other = lax.rem(q * 8 + chan + i, 32)
            second(chunk, other // 8, other % 8, q, chan).start()

    def arrive(chunk):
        @pl.loop(1, 32)
        def _(i):
            other = lax.rem(q * 8 + chan + 32 - i, 32)
            second(chunk, other // 8, other % 8, other // 8, other % 8).wait_recv()

    low = lax.broadcasted_iota(jnp.int32, (8, 128), 0) < 4

    def assemble(chunk):
        @pl.loop(0, PER // 2)
        def _(kp):
            rows = pl.ds(pl.multiple_of(kp * 16, 16), 16)
            for member in range(4):
                mx, mc = member // 2, member % 2
                for half in range(2):
                    parts = [
                        got[chunk, member, half * 4 + c, rows, :].astype(F32) for c in range(4)
                    ]
                    for kk in range(2):
                        v = [part[kk * 8 : kk * 8 + 8, :] for part in parts]
                        r = [pltpu.roll(x, 4, 0) for x in v]
                        re = jnp.concatenate(
                            [jnp.where(low, v[0], r[1]), jnp.where(low, v[2], r[3])], axis=0
                        )
                        im = jnp.concatenate(
                            [jnp.where(low, r[0], v[1]), jnp.where(low, r[2], v[3])], axis=0
                        )
                        at = pl.ds(mc * 32 + half * 16, 16)
                        channel = chunk * PER + kp * 2 + kk
                        gather[channel, mx, z, at, 0:128] = re.astype(BF16)
                        gather[channel, mx, z, at, 128:256] = im.astype(BF16)

    def is_kept(j):
        return (j == 1) | (j == 4)

    def mixed_at(j):
        return STEP * jnp.maximum(j - 1, 0)

    def kept_at(j):
        return 2 * (j // 4)

    def split(step):
        return step // SUBS, lax.rem(step, SUBS)

    def channel_of(step):
        chunk, j = split(step)
        return chunk * PER + jnp.where(is_kept(j), MIXED + kept_at(j), mixed_at(j))

    def shift(step, owner, to, way):
        first_one = channel_of(step) + (STEP // 2 if way == 3 else 0)
        block = gather.at[pl.ds(first_one, STEP if way < 2 else STEP // 2), :, owner]
        return pltpu.make_async_remote_copy(
            src_ref=block, dst_ref=block, send_sem=sz.at[way, step], recv_sem=rz.at[way, step],
            device_id=(plane_tile(q, to), chan), device_id_type=MESH,
        )

    def mixed_rows(chunk, j, src):
        return out.at[:, pl.ds(chunk * GROUP + MIXED * src + mixed_at(j), STEP)]

    def mixed_part(chunk, j, to):
        return obm.at[to, :, pl.ds(chunk * MIXED + mixed_at(j), STEP)]

    def spread(chunk, j, to, src):
        at = chunk * (MIXED // STEP) + mixed_at(j) // STEP
        return pltpu.make_async_remote_copy(
            src_ref=mixed_part(chunk, j, to), dst_ref=mixed_rows(chunk, j, src),
            send_sem=sm.at[to, at], recv_sem=rm.at[src, at],
            device_id=(plane_tile(to, z), chan), device_id_type=MESH,
        )

    def spread_own(chunk, j):
        return pltpu.make_async_copy(
            mixed_part(chunk, j, q), mixed_rows(chunk, j, q), lsem.at[chunk * SUBS + j]
        )

    def kept_rows(chunk, j, src):
        return out.at[:, pl.ds(chunk * GROUP + 4 * MIXED + KEPT * src + kept_at(j), STEP)]

    def kept_part(chunk, j, to):
        return obk.at[to, :, pl.ds(chunk * KEPT + kept_at(j), STEP)]

    def pair(chunk, j, src):
        at = chunk * (KEPT // STEP) + kept_at(j) // STEP
        return pltpu.make_async_remote_copy(
            src_ref=kept_part(chunk, j, 1 - core), dst_ref=kept_rows(chunk, j, src),
            send_sem=sk.at[at], recv_sem=rk.at[at],
            device_id=(plane_tile(x_lo * 2 + 1 - core, z), chan), device_id_type=MESH,
        )

    def pair_own(chunk, j):
        return pltpu.make_async_copy(
            kept_part(chunk, j, core), kept_rows(chunk, j, core), lsem.at[chunk * SUBS + j]
        )

    def correlate(mine, right):
        re, im = mine[:, :128], mine[:, 128:]
        left = jnp.concatenate([mine, jnp.concatenate([im, -re], axis=1)], axis=0)
        vis = lax.dot_general(left, right, (((1,), (1,)), ((), ())), preferred_element_type=F32)
        return (vis * (1.0 / SPEC)).astype(BF16)

    @pl.loop(0, EARLY)
    def _(chunk):
        dft(chunk)

    @pl.loop(0, NSUB + AHEAD + LAG)
    def _(tick):
        @pl.when(tick < NSUB)
        def _():
            chunk, j = split(tick)

            @pl.when(j == 0)
            def _():
                arrive(chunk)
                assemble(chunk)

            shift(tick, z, up, 0).start()
            shift(tick, z, down, 1).start()

        @pl.when((lax.rem(tick, GAP) == 0) & (tick // GAP < CHUNKS - EARLY))
        def _():
            dft(tick // GAP + EARLY)

        step = tick - AHEAD

        @pl.when((step >= 0) & (step < NSUB))
        def _():
            shift(step, down, up, 0).wait_recv()
            shift(step, up, down, 1).wait_recv()

            shift(step, down, up, 2).start()
            shift(step, up, down, 3).start()

        @pl.when(step >= LAG)
        def _():
            done = step - LAG
            shift(done, far, up, 2).wait_recv()
            shift(done, far, down, 3).wait_recv()
            chunk, j = split(done)
            base = channel_of(done)

            @pl.when(jnp.logical_not(is_kept(j)))
            def _():
                for kk in range(STEP):
                    mine = gather[base + kk, :, z].reshape(128, 256)
                    vis = correlate(mine, gather[base + kk].reshape(INPUTS, 256))
                    for to in range(4):
                        for p in range(2):
                            first_row = p * 128 + to * 32
                            obm[to, p, chunk * MIXED + mixed_at(j) + kk] = vis[first_row : first_row + 32, :]
                for m in (0, 1):
                    spread(chunk, j, (1 - x_lo) * 2 + lax.rem(core + m, 2), q).start()
                spread(chunk, j, x_lo * 2 + 1 - core, q).start()
                spread_own(chunk, j).start()

            @pl.when(is_kept(j))
            def _():
                for kk in range(STEP):
                    mine = gather[base + kk, x_lo, z]
                    vis = correlate(mine, gather[base + kk].reshape(INPUTS, 256))
                    for to in range(2):
                        for p in range(2):
                            first_row = p * 64 + to * 32
                            obk[to, p, chunk * KEPT + kept_at(j) + kk] = vis[first_row : first_row + 32, :]
                pair(chunk, j, core).start()
                pair_own(chunk, j).start()

    @pl.loop(0, RC)
    def _(r):
        @pl.loop(1, CHAN)
        def _(i):
            first(i, r).wait_send()

    @pl.loop(0, CHUNKS)
    def _(chunk):
        @pl.loop(1, 32)
        def _(i):
            other = lax.rem(q * 8 + chan + i, 32)
            second(chunk, other // 8, other % 8, q, chan).wait_send()

    @pl.loop(0, NSUB)
    def _(step):
        shift(step, z, up, 0).wait_send()
        shift(step, z, down, 1).wait_send()
        shift(step, down, up, 2).wait_send()
        shift(step, up, down, 3).wait_send()
        chunk, j = split(step)

        @pl.when(jnp.logical_not(is_kept(j)))
        def _():
            spread_own(chunk, j).wait()
            for m in (1, 2, 3):
                other = lax.rem(q + m, 4)
                spread(chunk, j, other, q).wait_send()
                spread(chunk, j, other, other).wait_recv()

        @pl.when(is_kept(j))
        def _():
            pair_own(chunk, j).wait()
            pair(chunk, j, core).wait_send()
            pair(chunk, j, 1 - core).wait_recv()


def widen(vis, out, wide, sem):
    per_part = CHUNKS * GROUP // WIDE

    def store(block):
        slot = lax.rem(block, SLOTS)
        return pltpu.make_async_copy(
            wide.at[slot],
            out.at[block // per_part, pl.ds(lax.rem(block, per_part) * WIDE, WIDE)],
            sem.at[slot],
        )

    @pl.loop(0, 2 * per_part)
    def _(block):
        @pl.when(block >= SLOTS)
        def _():
            store(block - SLOTS).wait()

        rows = pl.ds(lax.rem(block, per_part) * WIDE, WIDE)
        wide[lax.rem(block, SLOTS)] = vis[block // per_part, rows].astype(F32)
        store(block).start()

    @pl.loop(2 * per_part - SLOTS, 2 * per_part)
    def _(block):
        store(block).wait()


VM = pl.BlockSpec(memory_space=pltpu.VMEM)
ANY = pl.BlockSpec(memory_space=pl.ANY)
DMA = pltpu.SemaphoreType.DMA


def body(voltages, history, filter_taps):
    fine, coarse = (jnp.asarray(x) for x in phase_tables())
    vis = pl.pallas_call(
        kernel,
        name="correlator",
        out_shape=pltpu.VMEM((2, CHUNKS * GROUP, ROWS, INPUTS), BF16),
        in_specs=[ANY, ANY, VM, ANY, ANY],
        out_specs=VM,
        scratch_shapes=[
            pltpu.VMEM((SLOC, ROWS, FFT), jnp.int32),
            pltpu.VMEM((8, (TAPS - 1) * FFT), jnp.int32),
            pltpu.VMEM((2, CH, 128), F32),
            pltpu.VMEM((2, NT, 16, 128), F32),
            pltpu.VMEM((2 * CH, FFT), BF16),
            pltpu.VMEM((ROWS * SLOC, 128), F32),
            pltpu.VMEM((128, 128), F32),
            pltpu.VMEM((CHAN, NT, OWN * SLOC, 128), BF16),
            pltpu.VMEM((CHAN, NT, OWN * SLOC, 128), BF16),
            pltpu.VMEM((80 * 8, 128), F32),
            pltpu.VMEM((OWN * SPEC, FFT), BF16),
            pltpu.VMEM((OWN * SPEC, 128), F32),
            pltpu.VMEM((256 * 8, 128), F32),
            pltpu.VMEM((CHUNKS, CHAN, 4, PER * 8, 128), BF16),
            pltpu.VMEM((CHUNKS, 4, CHAN, PER * 8, 128), BF16),
            pltpu.VMEM((CHUNKS * PER, 2, 4, 64, 256), BF16),
            pltpu.VMEM((4, 2, CHUNKS * MIXED, ROWS, INPUTS), BF16),
            pltpu.VMEM((2, 2, CHUNKS * KEPT, ROWS, INPUTS), BF16),
            DMA((SLOC,)),
            DMA((3,)),
            DMA((RC, CHAN)),
            DMA((RC, CHAN)),
            DMA((CHUNKS, 4, CHAN)),
            DMA((CHUNKS, 4, CHAN)),
            DMA((4, NSUB)),
            DMA((4, NSUB)),
            DMA((4, CHUNKS * MIXED // 2)),
            DMA((4, CHUNKS * MIXED // 2)),
            DMA((CHUNKS * KEPT // 2,)),
            DMA((CHUNKS * KEPT // 2,)),
            DMA((NSUB,)),
        ],
        compiler_params=pltpu.CompilerParams(
            collective_id=0, has_side_effects=True, vmem_limit_bytes=LIMIT
        ),
    )(voltages, history, filter_taps, fine, coarse)
    return pl.pallas_call(
        widen,
        name="widen",
        out_shape=jax.ShapeDtypeStruct((2, CHUNKS * GROUP, ROWS, INPUTS), F32),
        in_specs=[VM],
        out_specs=ANY,
        scratch_shapes=[pltpu.VMEM((SLOTS, WIDE, ROWS, INPUTS), F32), DMA((SLOTS,))],
        compiler_params=pltpu.CompilerParams(vmem_limit_bytes=32 << 20),
    )(vis)


def solution(mesh):
    in_specs = (P("tile", "chan"), P("tile", None), P())
    out_specs = P(None, "chan", "tile", None)
    return jax.shard_map(body, mesh=mesh, in_specs=in_specs, out_specs=out_specs, check_vma=False)
```
